512 devices in a mesh: replica: 16 (over x, y_hi), shard: 32 (over y_lo, z, core).
Axes of the slice: x: 4, y: 8 (y_hi: 4, y_lo: 2; y = y_hi * 2 + y_lo), z: 8, core: 2. Of those that a mesh axis runs over, the one named last changes fastest.
Arguments:
- inputs: bfloat16 [131072, 6144], P(('replica', 'shard')), may hold values from -6 to 6
- doc_ids: int32 [512, 256], P(('replica', 'shard')), may hold values from 0 to 7, never falling along the last dimension, each value on 1 to 64 neighbouring positions
- values: bfloat16 [131072, 128], P(('replica', 'shard')), may hold values from -6 to 6
- cotangent: bfloat16 [131072, 128], P(('replica', 'shard')), may hold values from -24 to 24
- weights: float32 [98304, 256], P(('replica', 'shard')), may hold values from -6 to 6
- moment1: float32 [98304, 256], P(('replica', 'shard')), may hold values from -3 to 3
- moment2: float32 [98304, 256], P(('replica', 'shard')), may hold values from 0.05 to 2
- frag_local: bfloat16 [16, 16, 32, 6144], P('replica', None, 'shard'), may hold values from -6 to 6
- frag_global: float32 [16, 32, 6144], P(None, 'shard'), may hold values from -6 to 6
- frag_moment: float32 [16, 32, 6144], P(None, 'shard'), may hold values from -3 to 3
- frag_index: int32 [1], replicated, may hold values from 0 to 15
Outputs:
- new_weights: float32 [98304, 256], P(('replica', 'shard'))
- new_moment1: float32 [98304, 256], P(('replica', 'shard'))
- new_moment2: float32 [98304, 256], P(('replica', 'shard'))
- new_global: float32 [32, 6144], P('shard')
- new_moment: float32 [32, 6144], P('shard')
The draws below stay inside these ranges and needn't reach their ends.
Inputs may be any that keep to these rules, and one draw needn't show every extreme that they name: `doc_ids`: within each row document numbers start at 0, never fall, and each document has 1 to 64 tokens; some document has exactly 64.
All inputs are finite; a program needn't handle non-finite values.
Results may differ from the reference program's by a relative error of at most 0.008.
Values may be sent and summed in bfloat16 or wider, within the bound.
A program may use at most 64 MiB of HBM per device.

```python
import math
import jax
import jax.numpy as jnp
import numpy as np
from jax import lax

D = 6144
HEAD = 128
TOK_DEV = 256
FRAGS = 16
ADAM_STEP = 100
FRAG_ROWS = 32
TOKENS = 131072
SEQS = 512
N_REPLICA = 16
N_SHARD = 32


def block_levels(own_key, extent, cuts, least, high):
    def one(dim, parts):
        draws = jax.random.uniform(jax.random.fold_in(jax.random.fold_in(own_key, 6), dim), (parts,), jnp.float32, least / len(cuts), high / len(cuts))
        return jnp.repeat(jnp.exp(draws), extent[dim] // parts).reshape((-1,) + (1,) * (len(extent) - dim - 1))

    loudness = one(*cuts[0])
    for cut in cuts[1:]:
        loudness = loudness * one(*cut)
    return loudness


def profile(amount, total, most, slope):
    portions = [(1 << 20) // math.isqrt(rank ** slope) + 1 for rank in range(2, amount + 1)]
    rest, given = total - most - (amount - 1), [1] * (amount - 1)
    while rest > 0:
        free = [i for i in range(amount - 1) if given[i] < most]
        whole, budget = sum([portions[i] for i in free]), rest
        for i in free:
            more = min(most - given[i], max(1, budget * portions[i] // whole), rest)
            given[i] = given[i] + more
            rest = rest - more
    return np.array([most] + given)


def ragged_sizes(own_key, count, total, bound, lean):
    if count == 2:
        one = jax.random.randint(own_key, (), max(1, total - bound), min(bound, total - 1) + 1)
        return jnp.stack([one, total - one])
    tallies = jnp.asarray(profile(count, total, bound, lean), jnp.int32)
    couples = (count - 1) // 2
    source_of, taker = tallies[1:1 + 2 * couples:2], tallies[2:2 + 2 * couples:2]
    slack = jnp.minimum(source_of - 1, bound - taker)
    shifted = jax.random.randint(jax.random.fold_in(own_key, 1), (couples,), 0, 1 << 20) % (slack + 1)
    tallies = tallies.at[1:1 + 2 * couples:2].set(source_of - shifted).at[2:2 + 2 * couples:2].set(taker + shifted)
    return tallies[jax.random.permutation(jax.random.fold_in(own_key, 2), count)]


def bell_draw(own_key, dims, width, limit, split=(), kind=jnp.bfloat16):
    level = block_levels(own_key, dims, split, -0.22, 0.18) if split else 1.0
    values = jax.random.normal(own_key, dims, jnp.float32) * width * level
    return jnp.minimum(jnp.maximum(values, -limit), limit).astype(kind)


def setup_inputs(seed: int = 0) -> dict:
    keys = jax.random.split(jax.random.key(seed), 12)
    return {
        "inputs": bell_draw(keys[0], (TOKENS, D), 1.0, 6.0, ((0, 512),)),
        "doc_ids": jax.vmap(lambda own: jnp.searchsorted(jnp.cumsum(ragged_sizes(own, 8, TOK_DEV, TOK_DEV // 4, 1)), jnp.arange(TOK_DEV), side="right"))(jax.random.split(keys[1], SEQS)).reshape((SEQS, TOK_DEV)).astype(jnp.int32),
        "values": bell_draw(keys[2], (TOKENS, HEAD), 1.0, 6.0, ((0, 512),)),
        "cotangent": bell_draw(keys[3], (TOKENS, HEAD), 4.0, 24.0, ((0, 512),)),
        "weights": bell_draw(keys[4], (N_REPLICA * D, 2 * HEAD), 1.0, 6.0, ((0, 512),), jnp.float32),
        "moment1": bell_draw(keys[5], (N_REPLICA * D, 2 * HEAD), 0.5, 3.0, ((0, 512),), jnp.float32),
        "moment2": jnp.clip(jnp.exp(math.log(2.0) - 3.6888794 * jax.random.uniform(keys[6], (N_REPLICA * D, 2 * HEAD), jnp.float32) ** block_levels(keys[6], (N_REPLICA * D, 2 * HEAD), ((0, 512),), -0.2, 0.2)), 0.05, 2.0),
        "frag_local": bell_draw(keys[7], (N_REPLICA, FRAGS, FRAG_ROWS, D), 1.0, 6.0, ((0, 16), (2, 32))),
        "frag_global": bell_draw(keys[8], (FRAGS, FRAG_ROWS, D), 1.0, 6.0, ((1, 32),), jnp.float32),
        "frag_moment": bell_draw(keys[9], (FRAGS, FRAG_ROWS, D), 0.5, 3.0, ((1, 32),), jnp.float32),
        "frag_index": jax.random.randint(keys[10], (1,), 0, FRAGS).astype(jnp.int32),
    }


epsilon = 1e-06
beta_one = 0.9
beta_two = 0.95
learn_rate = 0.01
decay_rate = 0.1
outer_momentum = 0.9
outer_rate = 0.7

def head_grads(inputs, doc_ids, values, cotangent, projected):
    model_width = inputs.shape[1]
    head_size = values.shape[1]
    input_scale = 1.0 / math.sqrt(model_width)
    score_scale = 1.0 / math.sqrt(head_size)
    scaled = projected * input_scale
    queries = scaled[:, :head_size]
    keys_part = scaled[:, head_size:]
    q_rate = lax.rsqrt(lax.optimization_barrier(jnp.mean(queries * queries, axis=1, keepdims=True)) + epsilon)
    k_rate = lax.rsqrt(lax.optimization_barrier(jnp.mean(keys_part * keys_part, axis=1, keepdims=True)) + epsilon)
    q_unit = queries * q_rate
    k_unit = keys_part * k_rate
    scores = jnp.dot(q_unit, k_unit.T, precision=lax.Precision.HIGHEST) * score_scale
    position = jnp.arange(doc_ids.shape[0])
    allowed = (doc_ids[:, None] == doc_ids[None, :]) & (position[None, :] <= position[:, None])
    raised = jnp.where(allowed, jnp.exp(scores), jnp.float32(0.0))
    attention = raised / lax.optimization_barrier(jnp.sum(raised, axis=1, keepdims=True))
    grad_attention = jnp.dot(cotangent, values.T, preferred_element_type=jnp.float32)
    grad_scores = attention * (grad_attention - lax.optimization_barrier(jnp.sum(attention * grad_attention, axis=1, keepdims=True))) * score_scale
    grad_qunit = jnp.dot(grad_scores, k_unit, precision=lax.Precision.HIGHEST)
    grad_kunit = jnp.dot(grad_scores.T, q_unit, precision=lax.Precision.HIGHEST)
    grad_query = q_rate * (grad_qunit - q_unit * lax.optimization_barrier(jnp.mean(grad_qunit * q_unit, axis=1, keepdims=True)))
    grad_keys = k_rate * (grad_kunit - k_unit * lax.optimization_barrier(jnp.mean(grad_kunit * k_unit, axis=1, keepdims=True)))
    return (jnp.concatenate([grad_query, grad_keys], axis=1) * input_scale).astype(jnp.bfloat16)

def adam_update(weight_rows, first, second, gradient):
    first_new = beta_one * first + (1.0 - beta_one) * gradient
    second_new = beta_two * second + (1.0 - beta_two) * gradient * gradient
    first_hat = first_new / (1.0 - beta_one ** ADAM_STEP)
    second_hat = second_new / (1.0 - beta_two ** ADAM_STEP)
    weight_new = weight_rows - learn_rate * (first_hat / (jnp.sqrt(second_hat) + 1e-08) + decay_rate * weight_rows)
    return (weight_new, first_new, second_new)

def reference(inputs, doc_ids, values, cotangent, weights, moment1, moment2, frag_local, frag_global, frag_moment, frag_index):
    tok_all = inputs.reshape(N_REPLICA, N_SHARD, TOK_DEV, D)
    ids_all = doc_ids.reshape(N_REPLICA, N_SHARD, TOK_DEV)
    val_all = values.reshape(N_REPLICA, N_SHARD, TOK_DEV, HEAD)
    cot_all = cotangent.reshape(N_REPLICA, N_SHARD, TOK_DEV, HEAD)
    w_all = weights.reshape(N_REPLICA, D, 2 * HEAD)
    first_all = moment1.reshape(N_REPLICA, D, 2 * HEAD)
    second_all = moment2.reshape(N_REPLICA, D, 2 * HEAD)

    def replica_update(packed):
        tok_rep, ids_rep, val_rep, cot_rep, w_rep, first_rep, second_rep = packed
        lowered = w_rep.astype(jnp.bfloat16)

        def one_device(running, device):
            tok_dev, ids_dev, val_dev, cot_dev = device
            projected = jnp.dot(tok_dev, lowered, preferred_element_type=jnp.float32)
            grad_projected = head_grads(tok_dev, ids_dev, val_dev, cot_dev, projected)
            partial_term = lax.dot_general(tok_dev, grad_projected, (((0,), (0,)), ((), ())), preferred_element_type=jnp.float32)
            rounded = lax.optimization_barrier(partial_term.astype(jnp.bfloat16))
            return (running + rounded.astype(jnp.float32), None)
        start_sum = jnp.zeros((D, 2 * HEAD), jnp.float32)
        gradient, _ = lax.scan(one_device, start_sum, (tok_rep, ids_rep, val_rep, cot_rep))
        return adam_update(w_rep, first_rep, second_rep, gradient)
    new_w, new_first, new_second = lax.map(replica_update, (tok_all, ids_all, val_all, cot_all, w_all, first_all, second_all))
    new_weights = new_w.reshape(N_REPLICA * D, 2 * HEAD)
    new_moment1 = new_first.reshape(N_REPLICA * D, 2 * HEAD)
    new_moment2 = new_second.reshape(N_REPLICA * D, 2 * HEAD)
    chosen = frag_index[0].astype(jnp.int32)
    current = lax.dynamic_index_in_dim(frag_global, chosen, 0, keepdims=False)
    moment_now = lax.dynamic_index_in_dim(frag_moment, chosen, 0, keepdims=False)
    local_all = lax.dynamic_index_in_dim(frag_local, chosen, 1, keepdims=False)
    drift = lax.optimization_barrier((current[None] - local_all.astype(jnp.float32)).astype(jnp.bfloat16))
    drift_mean = lax.optimization_barrier(jnp.sum(drift.astype(jnp.float32), axis=0)) / N_REPLICA
    new_moment = outer_momentum * moment_now + drift_mean
    new_global = current - outer_rate * (drift_mean + outer_momentum * new_moment)
    return (new_weights, new_moment1, new_moment2, new_global, new_moment)
```

```python
import functools
import math

import jax
import jax.numpy as jnp
from jax import lax
from jax.experimental import pallas as pl
from jax.experimental.pallas import tpu as pltpu
from jax.sharding import PartitionSpec as P

ADAM_STEP = 100

epsilon = 1e-06
beta_one = 0.9
beta_two = 0.95
learn_rate = 0.01
decay_rate = 0.1
outer_momentum = 0.9
outer_rate = 0.7

Z = 8
DIRS = (1, -1)
KIND_A, KIND_B, KIND_O = 0, 1, 2
ORDER = (4, 3, -3, 2, -2, 1, -1, 0)


class Lanes:
    def __init__(self):
        self.numbers = {}

    def __call__(self, *key):
        return self.numbers.setdefault(key, len(self.numbers))


def kernel(
    n_x,
    n_y,
    lanes,
    index_ref,
    x_hbm,
    doc_hbm,
    val_hbm,
    cot_hbm,
    w_hbm,
    local_hbm,
    global_hbm,
    moment_hbm,
    grad_out,
    global_out,
    moment_out,
    x_buf,
    xt_buf,
    w_buf,
    gathered,
    proj,
    doc_buf,
    val_buf,
    cot_buf,
    allowed_buf,
    grad_att,
    gp_buf,
    local_buf,
    global_buf,
    moment_buf,
    drift_buf,
    x_recv,
    xsum_buf,
    y_recv,
    sums,
    chip_send,
    chip_recv,
    pair_send,
    pair_recv,
    ring_send,
    ring_recv,
    last_send,
    last_recv,
    load_sem,
    send_sem,
    recv_sem,
):
    tokens, width = x_buf.shape
    head = val_buf.shape[1]
    rows = width // (4 * Z)
    half, quarter = rows // 2, rows // 4

    replica = lax.axis_index("replica")
    shard = lax.axis_index("shard")
    my_x, my_y = replica // n_y, lax.rem(replica, n_y)
    side, z, core = shard // 16, lax.rem(shard // 2, Z), lax.rem(shard, 2)
    other = 1 - side

    def at_z(step):
        return lax.rem(z + step + 2 * Z, Z)

    def unit(col, zz, cc):
        return col * 16 + zz * 2 + cc

    to_core = {"shard": unit(side, z, 1 - core)}
    to_side = {"shard": unit(other, z, core)}
    to_z = {d: {"shard": unit(side, at_z(d), core)} for d in DIRS}
    to_x = [{"replica": lax.rem(my_x + k, n_x) * n_y + my_y} for k in range(1, n_x)]
    to_y = [{"replica": my_x * n_y + lax.rem(my_y + k, n_y)} for k in range(1, n_y)]

    started = []

    def send(key, src, dst, target):
        n = lanes(*key)
        copy = pltpu.make_async_remote_copy(
            src_ref=src,
            dst_ref=dst,
            send_sem=send_sem.at[n],
            recv_sem=recv_sem.at[n],
            device_id=target,
            device_id_type=pl.DeviceIdType.MESH,
        )
        copy.start()
        started.append(copy)

    def arrive(key, dst):
        n = lanes(*key)
        pltpu.make_async_remote_copy(
            src_ref=dst,
            dst_ref=dst,
            send_sem=send_sem.at[n],
            recv_sem=recv_sem.at[n],
            device_id=to_core,
            device_id_type=pl.DeviceIdType.MESH,
        ).wait_recv()

    def load(n, src, dst):
        copy = pltpu.make_async_copy(src, dst, load_sem.at[n])
        copy.start()
        return copy

    load_w = load(0, w_hbm, w_buf)
    load_local = load(1, local_hbm, local_buf)
    load_global = load(2, global_hbm, global_buf)
    load_x = load(3, x_hbm, x_buf)
    load_doc = load(4, doc_hbm, doc_buf)
    load_val = load(5, val_hbm, val_buf)
    load_cot = load(6, cot_hbm, cot_buf)
    load_moment = load(7, moment_hbm, moment_buf)

    barrier = pltpu.get_barrier_semaphore()
    partners = [to_core, to_side, to_z[1], to_z[-1]] + to_x + to_y
    for partner in partners:
        pl.semaphore_signal(
            barrier, inc=1, device_id=partner, device_id_type=pl.DeviceIdType.MESH
        )

    def span(col, zz, cc, lo, count):
        start = pl.multiple_of(unit(col, zz, cc) * rows + lo, 16)
        return gathered.at[pl.ds(start, count), :]

    load_w.wait()
    span(side, z, core, 0, rows)[...] = w_buf[...].astype(jnp.bfloat16)

    chosen = index_ref[0]
    load_local.wait()
    load_global.wait()
    current = global_buf[chosen]
    local_rows = local_buf[...].astype(jnp.float32)
    picked = lax.broadcasted_iota(jnp.int32, local_rows.shape, 0) == chosen
    local_copy = jnp.sum(jnp.where(picked, local_rows, 0.0), axis=0, keepdims=True)
    drift_buf[...] = (current - local_copy).astype(jnp.bfloat16).astype(jnp.float32)

    pl.semaphore_wait(barrier, len(partners))

    def piece(kind, direction, d, cc):
        zz = at_z(-direction * d)
        col = other if kind == KIND_O else side
        lo = 0 if kind == KIND_A else half
        if d == 4:
            return span(col, zz, cc, lo + (0 if direction == 1 else quarter), quarter)
        return span(col, zz, cc, lo, half)

    def side_piece(direction, d, cc, col):
        zz = at_z(-direction * d)
        if d == 4:
            return span(col, zz, cc, 0 if direction == 1 else quarter, quarter)
        return span(col, zz, cc, 0, half)

    def ring_on(kind, direction, d):
        if d < 4:
            src = piece(kind, direction, d, core)
            if d == 3:
                zz = at_z(-direction * d)
                col = other if kind == KIND_O else side
                lo = 0 if kind == KIND_A else half
                src = span(col, zz, core, lo + (0 if direction == 1 else quarter), quarter)
            send(("ring", kind, direction, d + 1), src, src, to_z[direction])

    for direction in DIRS:
        ring_on(KIND_A, direction, 0)
    first_b = span(side, z, core, half, half)
    send(("sideB",), first_b, first_b, to_side)
    for direction in DIRS:
        ring_on(KIND_B, direction, 0)
    first_a = span(side, z, core, 0, half)
    send(("sideA", 0, 1), first_a, first_a, to_side)
    mine = span(side, z, core, 0, rows)
    send(("core", "own"), mine, mine, to_core)
    for k, target in enumerate(to_x):
        send(("x", k), drift_buf, x_recv.at[k], target)

    load_x.wait()
    block = 2 * rows

    def transpose_block(p):
        cols = slice(p * block, (p + 1) * block)
        xt_buf[cols, :] = x_buf[:, cols].T

    def make_allowed():
        load_doc.wait()
        by_column = jnp.broadcast_to(doc_buf[...], (tokens, tokens))
        by_row = by_column.T
        row = lax.broadcasted_iota(jnp.int32, (tokens, tokens), 0)
        column = lax.broadcasted_iota(jnp.int32, (tokens, tokens), 1)
        same = (by_row == by_column) & (column <= row)
        allowed_buf[...] = jnp.where(same, 1.0, 0.0)

    def make_grad_att():
        load_val.wait()
        load_cot.wait()
        grad_att[...] = lax.dot_general(
            cot_buf[...],
            val_buf[...],
            (((1,), (1,)), ((), ())),
            preferred_element_type=jnp.float32,
        )

    def multiply(col, zz, first=False):
        start = pl.multiple_of(unit(col, zz, 0) * rows, 128)
        term = jnp.dot(
            x_buf[:, pl.ds(start, block)],
            gathered[pl.ds(start, block), :],
            preferred_element_type=jnp.float32,
        )
        if first:
            proj[...] = term
        else:
            proj[...] += term

    def arrive_core(d):
        for direction in DIRS if d else (1,):
            if d == 0:
                arrive(("core", "own"), span(side, z, 1 - core, 0, rows))
                arrive(("core", "sideB"), span(other, z, 1 - core, half, half))
            else:
                for kind in (KIND_A, KIND_B, KIND_O):
                    arrive(
                        ("core", kind, direction, d), piece(kind, direction, d, 1 - core)
                    )
            arrive(
                ("core", "sideA", direction, d), side_piece(direction, d, 1 - core, other)
            )

    fillers = [functools.partial(transpose_block, p) for p in range(2 * Z)]
    fillers += [make_allowed, make_grad_att]

    def fill(count=1):
        for _ in range(min(count, len(fillers))):
            fillers.pop(0)()

    def queue_products(d):
        def first_of(d=d):
            arrive_core(d)

        fillers.append(first_of)
        for direction in DIRS if 0 < d < 4 else (1,):
            for col in (side, other):
                fillers.append(
                    functools.partial(
                        multiply, col, at_z(-direction * d), first=d == 0 and col is side
                    )
                )

    def sums_over_x():
        total = drift_buf[...]
        for k in range(n_x - 1):
            arrive(("x", k), x_recv.at[k])
            total = total + x_recv[k]
        xsum_buf[...] = total
        for k, target in enumerate(to_y):
            send(("y", k), xsum_buf, y_recv.at[k], target)

    arrive(("sideB",), span(other, z, core, half, half))
    for direction in DIRS:
        ring_on(KIND_O, direction, 0)
    their_b = span(other, z, core, half, half)
    send(("core", "sideB"), their_b, their_b, to_core)
    fill(4)
    for d in range(1, 5):
        for kind in (KIND_A, KIND_B, KIND_O):
            for direction in DIRS:
                got = piece(kind, direction, d, core)
                arrive(("ring", kind, direction, d), got)
                ring_on(kind, direction, d)
                if kind == KIND_A:
                    send(("sideA", d, direction), got, got, to_side)
                send(("core", kind, direction, d), got, got, to_core)
            if kind == KIND_A:
                for direction in DIRS if d > 1 else (1,):
                    got = side_piece(direction, d - 1, core, other)
                    arrive(("sideA", d - 1, direction), got)
                    send(("core", "sideA", direction, d - 1), got, got, to_core)
            fill(2)
        if d >= 2:
            queue_products(d - 2)
    sums_over_x()
    fill(len(fillers))
    for direction in DIRS:
        got = side_piece(direction, 4, core, other)
        arrive(("sideA", 4, direction), got)
        send(("core", "sideA", direction, 4), got, got, to_core)
    queue_products(3)
    queue_products(4)
    fill(len(fillers))

    input_scale = 1.0 / math.sqrt(width)
    score_scale = 1.0 / math.sqrt(head)
    exact = lax.Precision.HIGHEST
    scaled = proj[...] * input_scale
    queries, keys_part = scaled[:, :head], scaled[:, head:]
    q_rate = lax.rsqrt(jnp.mean(queries * queries, axis=1, keepdims=True) + epsilon)
    k_rate = lax.rsqrt(jnp.mean(keys_part * keys_part, axis=1, keepdims=True) + epsilon)
    q_unit, k_unit = queries * q_rate, keys_part * k_rate
    scores = (
        lax.dot_general(
            q_unit,
            k_unit,
            (((1,), (1,)), ((), ())),
            precision=exact,
            preferred_element_type=jnp.float32,
        )
        * score_scale
    )
    raised = jnp.where(allowed_buf[...] > 0.5, jnp.exp(scores), 0.0)
    attention = raised / jnp.sum(raised, axis=1, keepdims=True)
    weighted = attention * grad_att[...]
    grad_scores = (
        weighted - attention * jnp.sum(weighted, axis=1, keepdims=True)
    ) * score_scale
    grad_qunit = jnp.dot(
        grad_scores, k_unit, precision=exact, preferred_element_type=jnp.float32
    )
    grad_kunit = jnp.dot(
        grad_scores.T, q_unit, precision=exact, preferred_element_type=jnp.float32
    )
    grad_query = q_rate * (
        grad_qunit - q_unit * jnp.mean(grad_qunit * q_unit, axis=1, keepdims=True)
    )
    grad_keys = k_rate * (
        grad_kunit - k_unit * jnp.mean(grad_kunit * k_unit, axis=1, keepdims=True)
    )
    gp_buf[:, :head] = (grad_query * input_scale).astype(jnp.bfloat16)
    gp_buf[:, head:] = (grad_keys * input_scale).astype(jnp.bfloat16)

    def place(delta):
        return ORDER.index(delta)

    def partial(col, zz, cc):
        start = pl.multiple_of(unit(col, zz, cc) * rows, 64)
        return jnp.dot(
            xt_buf[pl.ds(start, rows), :], gp_buf[...], preferred_element_type=jnp.float32
        )

    def compute(delta):
        i, zz = place(delta), at_z(delta)
        for k, col in ((1, other), (0, side)):
            chip_send[i, k] = partial(col, zz, 1 - core).astype(jnp.bfloat16)
            send(("chip", i, k), chip_send.at[i, k], chip_recv.at[i, k], to_core)
        for k, col in ((1, other), (0, side)):
            sums[i, k] = partial(col, zz, core)

    def pair(delta):
        i = place(delta)
        for k in (1, 0):
            arrive(("chip", i, k), chip_recv.at[i, k])
            sums[i, k] += chip_recv[i, k].astype(jnp.float32)
            if k == 1:
                pair_send[i] = sums[i, 1, :half].astype(jnp.bfloat16)
                send(("pair", i), pair_send.at[i], pair_recv.at[i], to_side)

    def across(delta):
        i = place(delta)
        arrive(("pair", i), pair_recv.at[i])
        sums[i, 0, :half] += pair_recv[i].astype(jnp.float32)

    def early(direction):
        return 1 if direction == 1 else 0

    def slot(direction, kind, d, h):
        return ((0 if direction == 1 else 1) * 3 + kind) * 8 + (d - 1) * 2 + h

    def ring_sum(kind, direction, d, h):
        delta = 4 if d == 4 else direction * d
        k = 1 if kind == KIND_O else 0
        lo = (0 if kind == KIND_A else half) + h * quarter
        total = sums[place(delta), k, lo : lo + quarter]
        if d < 3 or (d == 3 and h != early(direction)):
            n = slot(direction, kind, d + 1, h)
            arrive(("sum", n), ring_recv.at[n])
            total = total + ring_recv[n].astype(jnp.float32)
        n = slot(direction, kind, d, h)
        ring_send[n] = total.astype(jnp.bfloat16)
        send(("sum", n), ring_send.at[n], ring_recv.at[n], to_z[direction])

    compute(4)
    compute(3)
    compute(-3)
    pair(4)
    for kind in (KIND_O, KIND_B):
        for direction in DIRS:
            ring_sum(kind, direction, 4, 1 - early(direction))
    for direction in DIRS:
        pair(3 * direction)
        for kind in (KIND_O, KIND_B):
            ring_sum(kind, direction, 3, early(direction))
    compute(2)
    across(4)
    for direction in DIRS:
        ring_sum(KIND_A, direction, 4, 1 - early(direction))
    compute(-2)
    for direction in DIRS:
        across(3 * direction)
        ring_sum(KIND_A, direction, 3, early(direction))
    pair(2)
    pair(-2)
    compute(1)
    compute(-1)
    for kind in (KIND_O, KIND_B, KIND_A):
        for direction in DIRS:
            ring_sum(kind, direction, 3, 1 - early(direction))
    pair(1)
    pair(-1)
    compute(0)
    across(2)
    across(-2)
    for first in (True, False):
        for kind in (KIND_O, KIND_B, KIND_A):
            for direction in DIRS:
                h = early(direction) if first else 1 - early(direction)
                ring_sum(kind, direction, 2, h)
    pair(0)
    across(1)
    across(-1)
    for first in (True, False):
        for kind in (KIND_O, KIND_B, KIND_A):
            for direction in DIRS:
                h = early(direction) if first else 1 - early(direction)
                ring_sum(kind, direction, 1, h)

    load_moment.wait()
    total = xsum_buf[...]
    for k in range(n_y - 1):
        arrive(("y", k), y_recv.at[k])
        total = total + y_recv[k]
    drift_mean = total / (n_x * n_y)
    new_moment = outer_momentum * moment_buf[chosen] + drift_mean
    moment_out[...] = new_moment
    global_out[...] = global_buf[chosen] - outer_rate * (
        drift_mean + outer_momentum * new_moment
    )

    across(0)

    def last_sum(kind, h):
        k = 1 if kind == KIND_O else 0
        lo = (0 if kind == KIND_A else half) + h * quarter
        total = sums[place(0), k, lo : lo + quarter]
        for direction in DIRS:
            n = slot(direction, kind, 1, h)
            arrive(("sum", n), ring_recv.at[n])
            total = total + ring_recv[n].astype(jnp.float32)
        return total

    for h in (0, 1):
        last_send[h] = last_sum(KIND_O, h).astype(jnp.bfloat16)
        send(("last", h), last_send.at[h], last_recv.at[h], to_side)
    for h in (0, 1):
        grad_out[pl.ds(h * quarter, quarter), :] = last_sum(KIND_A, h)
    for h in (0, 1):
        total = last_sum(KIND_B, h)
        arrive(("last", h), last_recv.at[h])
        grad_out[pl.ds(half + h * quarter, quarter), :] = total + last_recv[h].astype(
            jnp.float32
        )
    for copy in started:
        copy.wait_send()


def exchange(n_replica, inputs, doc_ids, values, cotangent, weights, local, current, moment, index):
    tokens, width = inputs.shape
    head = values.shape[1]
    rows = width // (4 * Z)
    half, quarter = rows // 2, rows // 4
    n_x = min(4, n_replica)
    n_y = n_replica // n_x
    bf16, f32 = jnp.bfloat16, jnp.float32
    anywhere = pl.BlockSpec(memory_space=pl.ANY)
    vmem = pl.BlockSpec(memory_space=pltpu.VMEM)
    n_sem = 192
    return pl.pallas_call(
        functools.partial(kernel, n_x, n_y, Lanes()),
        out_shape=(
            jax.ShapeDtypeStruct((rows, 2 * head), f32),
            jax.ShapeDtypeStruct((1, width), f32),
            jax.ShapeDtypeStruct((1, width), f32),
        ),
        in_specs=[pl.BlockSpec(memory_space=pltpu.SMEM)] + [anywhere] * 8,
        out_specs=(vmem, vmem, vmem),
        scratch_shapes=[
            pltpu.VMEM((tokens, width), bf16),
            pltpu.VMEM((width, tokens), bf16),
            pltpu.VMEM((rows, 2 * head), f32),
            pltpu.VMEM((width, 2 * head), bf16),
            pltpu.VMEM((tokens, 2 * head), f32),
            pltpu.VMEM((1, tokens), jnp.int32),
            pltpu.VMEM((tokens, head), bf16),
            pltpu.VMEM((tokens, head), bf16),
            pltpu.VMEM((tokens, tokens), f32),
            pltpu.VMEM((tokens, tokens), f32),
            pltpu.VMEM((tokens, 2 * head), bf16),
            pltpu.VMEM(local.shape, bf16),
            pltpu.VMEM(current.shape, f32),
            pltpu.VMEM(moment.shape, f32),
            pltpu.VMEM((1, width), f32),
            pltpu.VMEM((max(n_x - 1, 1), 1, width), f32),
            pltpu.VMEM((1, width), f32),
            pltpu.VMEM((max(n_y - 1, 1), 1, width), f32),
            pltpu.VMEM((8, 2, rows, 2 * head), f32),
            pltpu.VMEM((8, 2, rows, 2 * head), bf16),
            pltpu.VMEM((8, 2, rows, 2 * head), bf16),
            pltpu.VMEM((8, half, 2 * head), bf16),
            pltpu.VMEM((8, half, 2 * head), bf16),
            pltpu.VMEM((48, quarter, 2 * head), bf16),
            pltpu.VMEM((48, quarter, 2 * head), bf16),
            pltpu.VMEM((2, quarter, 2 * head), bf16),
            pltpu.VMEM((2, quarter, 2 * head), bf16),
            pltpu.SemaphoreType.DMA((8,)),
            pltpu.SemaphoreType.DMA((n_sem,)),
            pltpu.SemaphoreType.DMA((n_sem,)),
        ],
        compiler_params=pltpu.CompilerParams(
            collective_id=0, has_side_effects=True, vmem_limit_bytes=56 * 1024 * 1024
        ),
    )(index, inputs, doc_ids, values, cotangent, weights, local, current, moment)


def on_device(
    n_replica,
    inputs,
    doc_ids,
    values,
    cotangent,
    weights,
    moment1,
    moment2,
    frag_local,
    frag_global,
    frag_moment,
    frag_index,
):
    gradient, new_global, new_moment = exchange(
        n_replica,
        inputs,
        doc_ids,
        values,
        cotangent,
        weights,
        frag_local[0, :, 0, :],
        frag_global,
        frag_moment,
        frag_index,
    )
    first_new = beta_one * moment1 + (1.0 - beta_one) * gradient
    second_new = beta_two * moment2 + (1.0 - beta_two) * gradient * gradient
    first_hat = first_new / (1.0 - beta_one**ADAM_STEP)
    second_hat = second_new / (1.0 - beta_two**ADAM_STEP)
    weight_new = weights - learn_rate * (
        first_hat / (jnp.sqrt(second_hat) + 1e-08) + decay_rate * weights
    )
    return (weight_new, first_new, second_new, new_global, new_moment)


def solution(mesh):
    both = P(("replica", "shard"), None)
    return jax.shard_map(
        functools.partial(on_device, mesh.shape["replica"]),
        mesh=mesh,
        in_specs=(both,) * 7
        + (
            P("replica", None, "shard", None),
            P(None, "shard", None),
            P(None, "shard", None),
            P(),
        ),
        out_specs=(both, both, both, P("shard", None), P("shard", None)),
        check_vma=False,
    )
```

```python
import functools
import math

import jax
import jax.numpy as jnp
from jax import lax
from jax.experimental import pallas as pl
from jax.experimental.pallas import tpu as pltpu
from jax.sharding import PartitionSpec as P

ADAM_STEP = 100

epsilon = 1e-06
beta_one = 0.9
beta_two = 0.95
learn_rate = 0.01
decay_rate = 0.1
outer_momentum = 0.9
outer_rate = 0.7

Z = 8
DIRS = (1, -1)
KIND_A, KIND_B, KIND_O = 0, 1, 2
RING, SIDE, CORE, CHIP, PAIR, SUM, LAST, ACROSS_X, ACROSS_Y = range(9)
ORDER = (4, 3, -3, 2, -2, 1, -1, 0)


class Lanes:
    def __init__(self):
        self.numbers = {}

    def __call__(self, *key):
        return self.numbers.setdefault(key, len(self.numbers))


def kernel(
    n_x,
    n_y,
    lanes,
    index_hbm,
    x_hbm,
    doc_hbm,
    val_hbm,
    cot_hbm,
    w_hbm,
    local_hbm,
    global_hbm,
    moment_hbm,
    grad_out,
    global_out,
    moment_out,
    index_buf,
    x_buf,
    xt_buf,
    w_buf,
    gathered,
    proj,
    doc_buf,
    val_buf,
    cot_buf,
    allowed_buf,
    grad_att,
    gp_buf,
    local_buf,
    global_buf,
    moment_buf,
    drift_buf,
    x_recv,
    xsum_buf,
    y_recv,
    sums,
    chip_send,
    chip_recv,
    pair_send,
    pair_recv,
    ring_send,
    ring_recv,
    last_send,
    last_recv,
    load_sem,
    send_sem,
    recv_sem,
):
    tokens, width = x_buf.shape
    head = val_buf.shape[1]
    rows = width // (4 * Z)
    half, quarter = rows // 2, rows // 4

    replica = lax.axis_index("replica")
    shard = lax.axis_index("shard")
    my_x, my_y = replica // n_y, lax.rem(replica, n_y)
    side, z, core = shard // 16, lax.rem(shard // 2, Z), lax.rem(shard, 2)
    other = 1 - side

    def at_z(step):
        return lax.rem(z + step + 2 * Z, Z)

    def unit(col, zz, cc):
        return col * 16 + zz * 2 + cc

    to_core = {"shard": unit(side, z, 1 - core)}
    to_side = {"shard": unit(other, z, core)}
    to_z = {d: {"shard": unit(side, at_z(d), core)} for d in DIRS}
    to_x = [{"replica": lax.rem(my_x + k, n_x) * n_y + my_y} for k in range(1, n_x)]
    to_y = [{"replica": my_x * n_y + lax.rem(my_y + k, n_y)} for k in range(1, n_y)]

    def describe(stream, key, src, dst, target):
        return pltpu.make_async_remote_copy(
            src_ref=src,
            dst_ref=dst,
            send_sem=send_sem.at[stream],
            recv_sem=recv_sem.at[lanes(*key)],
            device_id=target,
            device_id_type=pl.DeviceIdType.MESH,
        )

    def send(stream, key, src, dst, target):
        describe(stream, key, src, dst, target).start()

    def arrive(key, dst):
        describe(0, key, dst, dst, to_core).wait_recv()

    def drain(stream, src):
        describe(stream, ("core", 0), src, src, to_core).wait_send()

    barrier = pltpu.get_barrier_semaphore()
    partners = [to_core, to_side, to_z[1], to_z[-1]] + to_x + to_y
    for partner in partners:
        pl.semaphore_signal(
            barrier, inc=1, device_id=partner, device_id_type=pl.DeviceIdType.MESH
        )

    def load(n, src, dst):
        copy = pltpu.make_async_copy(src, dst, load_sem.at[n])
        copy.start()
        return copy

    load_w = load(0, w_hbm, w_buf)
    load_local = load(1, local_hbm, local_buf)
    load_global = load(2, global_hbm, global_buf)
    load_x = load(3, x_hbm, x_buf)
    load_doc = load(4, doc_hbm, doc_buf)
    load_val = load(5, val_hbm, val_buf)
    load_cot = load(6, cot_hbm, cot_buf)
    load_moment = load(7, moment_hbm, moment_buf)
    load_index = load(8, index_hbm, index_buf)

    def span(col, zz, cc, lo, count):
        start = pl.multiple_of(unit(col, zz, cc) * rows + lo, 16)
        return gathered.at[pl.ds(start, count), :]

    load_w.wait()
    span(side, z, core, 0, rows)[...] = w_buf[...].astype(jnp.bfloat16)

    load_index.wait()
    chosen = index_buf[0]
    load_local.wait()
    load_global.wait()
    current = global_buf[chosen]
    local_rows = local_buf[...].astype(jnp.float32)
    picked = lax.broadcasted_iota(jnp.int32, local_rows.shape, 0) == chosen
    local_copy = jnp.sum(jnp.where(picked, local_rows, 0.0), axis=0, keepdims=True)
    drift_buf[...] = (current - local_copy).astype(jnp.bfloat16).astype(jnp.float32)

    pl.semaphore_wait(barrier, len(partners))

    def piece(kind, direction, d, cc):
        zz = at_z(-direction * d)
        col = other if kind == KIND_O else side
        lo = 0 if kind == KIND_A else half
        if d == 4:
            return span(col, zz, cc, lo + (0 if direction == 1 else quarter), quarter)
        return span(col, zz, cc, lo, half)

    def side_piece(direction, d, cc, col):
        zz = at_z(-direction * d)
        if d == 4:
            return span(col, zz, cc, 0 if direction == 1 else quarter, quarter)
        return span(col, zz, cc, 0, half)

    def ring_on(kind, direction, d):
        if d < 4:
            src = piece(kind, direction, d, core)
            if d == 3:
                zz = at_z(-direction * d)
                col = other if kind == KIND_O else side
                lo = 0 if kind == KIND_A else half
                src = span(col, zz, core, lo + (0 if direction == 1 else quarter), quarter)
            send(RING, ("ring", kind, direction, d + 1), src, src, to_z[direction])

    def side_on(d, got):
        send(SIDE, ("side", d), got, got, to_side)

    def core_on(d, got):
        send(CORE, ("core", d), got, got, to_core)

    first_a = span(side, z, core, 0, half)
    first_b = span(side, z, core, half, half)
    their_b = span(other, z, core, half, half)
    for direction in DIRS:
        ring_on(KIND_A, direction, 0)
    send(SIDE, ("sideB",), first_b, first_b, to_side)
    for direction in DIRS:
        ring_on(KIND_B, direction, 0)
    side_on(0, first_a)
    core_on(0, span(side, z, core, 0, rows))
    for k, target in enumerate(to_x):
        send(ACROSS_X, ("x",), drift_buf, x_recv.at[k], target)

    load_x.wait()
    block = 2 * rows

    def transpose_block(p):
        cols = slice(p * block, (p + 1) * block)
        turned = x_buf[:, cols].T
        for cc in (0, 1):
            start = pl.multiple_of(p * block + (core if cc == 0 else 1 - core) * rows, 64)
            xt_buf[pl.ds(start, rows), :] = turned[cc * rows : (cc + 1) * rows]

    def make_allowed():
        load_doc.wait()
        by_column = jnp.broadcast_to(doc_buf[...], (tokens, tokens))
        by_row = by_column.T
        row = lax.broadcasted_iota(jnp.int32, (tokens, tokens), 0)
        column = lax.broadcasted_iota(jnp.int32, (tokens, tokens), 1)
        same = (by_row == by_column) & (column <= row)
        allowed_buf[...] = jnp.where(same, 1.0, 0.0)

    def make_grad_att():
        load_val.wait()
        load_cot.wait()
        grad_att[...] = lax.dot_general(
            cot_buf[...],
            val_buf[...],
            (((1,), (1,)), ((), ())),
            preferred_element_type=jnp.float32,
        )

    def multiply(col, zz, first=False):
        start = pl.multiple_of(unit(col, zz, 0) * rows, 128)
        term = jnp.dot(
            x_buf[:, pl.ds(start, block)],
            gathered[pl.ds(start, block), :],
            preferred_element_type=jnp.float32,
        )
        if first:
            proj[...] = term
        else:
            proj[...] += term

    def arrive_core(d):
        count = 2 * rows if d in (0, 4) else 4 * rows
        arrive(("core", d), gathered.at[pl.ds(0, count), :])

    fillers = [functools.partial(transpose_block, p) for p in range(2 * Z)]
    fillers += [make_allowed, make_grad_att]

    def fill(count=1):
        for _ in range(min(count, len(fillers))):
            fillers.pop(0)()

    def queue_products(d):
        fillers.append(functools.partial(arrive_core, d))
        for direction in DIRS if 0 < d < 4 else (1,):
            for col in (side, other):
                fillers.append(
                    functools.partial(
                        multiply, col, at_z(-direction * d), first=d == 0 and col is side
                    )
                )

    def sums_over_x():
        total = drift_buf[...]
        if n_x > 1:
            arrive(("x",), x_recv)
        for k in range(n_x - 1):
            total = total + x_recv[k]
        xsum_buf[...] = total
        for k, target in enumerate(to_y):
            send(ACROSS_Y, ("y",), xsum_buf, y_recv.at[k], target)

    def from_side(d):
        arrive(("side", d), gathered.at[pl.ds(0, half if d in (0, 4) else rows), :])
        for direction in DIRS if d else (1,):
            core_on(d, side_piece(direction, d, core, other))

    def from_ring(kind, d):
        for direction in DIRS:
            got = piece(kind, direction, d, core)
            arrive(("ring", kind, direction, d), got)
            ring_on(kind, direction, d)
            if kind == KIND_A:
                side_on(d, got)
            core_on(d, got)

    fill(2)
    for d in range(1, 5):
        from_ring(KIND_A, d)
        from_ring(KIND_B, d)
        if d == 1:
            arrive(("sideB",), their_b)
            for direction in DIRS:
                ring_on(KIND_O, direction, 0)
            core_on(0, their_b)
        else:
            from_ring(KIND_O, d - 1)
        fill(3)
        from_side(d - 1)
        fill(3)
        queue_products(d - 1)
    sums_over_x()
    from_side(4)
    from_ring(KIND_O, 4)
    queue_products(4)
    fill(len(fillers))

    input_scale = 1.0 / math.sqrt(width)
    score_scale = 1.0 / math.sqrt(head)
    exact = lax.Precision.HIGHEST
    scaled = proj[...] * input_scale
    queries, keys_part = scaled[:, :head], scaled[:, head:]
    q_rate = lax.rsqrt(jnp.mean(queries * queries, axis=1, keepdims=True) + epsilon)
    k_rate = lax.rsqrt(jnp.mean(keys_part * keys_part, axis=1, keepdims=True) + epsilon)
    q_unit, k_unit = queries * q_rate, keys_part * k_rate
    scores = (
        lax.dot_general(
            q_unit,
            k_unit,
            (((1,), (1,)), ((), ())),
            precision=exact,
            preferred_element_type=jnp.float32,
        )
        * score_scale
    )
    raised = jnp.where(allowed_buf[...] > 0.5, jnp.exp(scores), 0.0)
    attention = raised / jnp.sum(raised, axis=1, keepdims=True)
    weighted = attention * grad_att[...]
    grad_scores = (
        weighted - attention * jnp.sum(weighted, axis=1, keepdims=True)
    ) * score_scale
    grad_qunit = jnp.dot(
        grad_scores, k_unit, precision=exact, preferred_element_type=jnp.float32
    )
    grad_kunit = jnp.dot(
        grad_scores.T, q_unit, precision=exact, preferred_element_type=jnp.float32
    )
    grad_query = q_rate * (
        grad_qunit - q_unit * jnp.mean(grad_qunit * q_unit, axis=1, keepdims=True)
    )
    grad_keys = k_rate * (
        grad_kunit - k_unit * jnp.mean(grad_kunit * k_unit, axis=1, keepdims=True)
    )
    gp_buf[:, :head] = (grad_query * input_scale).astype(jnp.bfloat16)
    gp_buf[:, head:] = (grad_keys * input_scale).astype(jnp.bfloat16)

    def place(delta):
        return ORDER.index(delta)

    def compute(delta):
        i, zz = place(delta), at_z(delta)
        for k, col in ((1, other), (0, side)):
            start = pl.multiple_of(unit(col, zz, 0) * rows, 128)
            term = jnp.dot(
                xt_buf[pl.ds(start, block), :],
                gp_buf[...],
                preferred_element_type=jnp.float32,
            )
            chip_send[i, k] = term[rows:].astype(jnp.bfloat16)
            sums[i, k] = term[:rows]
        send(CHIP, ("chip", i), chip_send.at[i], chip_recv.at[i], to_core)

    def pair(delta):
        i = place(delta)
        arrive(("chip", i), chip_recv.at[i])
        for k in (1, 0):
            sums[i, k] += chip_recv[i, k].astype(jnp.float32)
            if k == 1:
                pair_send[i] = sums[i, 1, :half].astype(jnp.bfloat16)
                send(PAIR, ("pair", i), pair_send.at[i], pair_recv.at[i], to_side)

    def across(delta):
        i = place(delta)
        arrive(("pair", i), pair_recv.at[i])
        sums[i, 0, :half] += pair_recv[i].astype(jnp.float32)

    def early(direction):
        return 1 if direction == 1 else 0

    def slot(direction, kind, d, h):
        return ((0 if direction == 1 else 1) * 3 + kind) * 8 + (d - 1) * 2 + h

    def ring_sum(kind, direction, d, h):
        delta = 4 if d == 4 else direction * d
        k = 1 if kind == KIND_O else 0
        lo = (0 if kind == KIND_A else half) + h * quarter
        total = sums[place(delta), k, lo : lo + quarter]
        if d < 3 or (d == 3 and h != early(direction)):
            n = slot(direction, kind, d + 1, h)
            arrive(("sum", n), ring_recv.at[n])
            total = total + ring_recv[n].astype(jnp.float32)
        n = slot(direction, kind, d, h)
        ring_send[n] = total.astype(jnp.bfloat16)
        send(SUM, ("sum", n), ring_send.at[n], ring_recv.at[n], to_z[direction])

    def sum_on(kinds, d, first, directions=DIRS):
        for kind in kinds:
            for direction in directions:
                h = early(direction) if first else 1 - early(direction)
                ring_sum(kind, direction, d, h)

    whole, split = (KIND_O, KIND_B), (KIND_A,)
    compute(4)
    compute(3)
    pair(4)
    sum_on(whole, 4, False)
    compute(-3)
    pair(3)
    sum_on(whole, 3, True, (1,))
    compute(2)
    pair(-3)
    sum_on(whole, 3, True, (-1,))
    compute(-2)
    pair(2)
    sum_on(whole, 3, False)
    compute(1)
    pair(-2)
    across(4)
    sum_on(split, 4, False)
    sum_on(whole, 2, True)
    compute(-1)
    pair(1)
    across(3)
    across(-3)
    sum_on(split, 3, True)
    compute(0)
    pair(-1)
    sum_on(whole, 2, False)
    sum_on(split, 3, False)
    pair(0)
    sum_on(whole, 1, True)
    across(2)
    across(-2)
    sum_on(split, 2, True)
    sum_on(whole, 1, False)
    sum_on(split, 2, False)
    across(1)
    across(-1)
    sum_on(split, 1, True)
    sum_on(split, 1, False)

    load_moment.wait()
    total = xsum_buf[...]
    if n_y > 1:
        arrive(("y",), y_recv)
    for k in range(n_y - 1):
        total = total + y_recv[k]
    drift_mean = total / (n_x * n_y)
    new_moment = outer_momentum * moment_buf[chosen] + drift_mean
    new_global = global_buf[chosen] - outer_rate * (
        drift_mean + outer_momentum * new_moment
    )
    for j in range(width // 128):
        lane = slice(j * 128, (j + 1) * 128)
        moment_out[j : j + 1, :] = new_moment[:, lane]
        global_out[j : j + 1, :] = new_global[:, lane]

    across(0)

    def last_sum(kind, h):
        k = 1 if kind == KIND_O else 0
        lo = (0 if kind == KIND_A else half) + h * quarter
        total = sums[place(0), k, lo : lo + quarter]
        for direction in DIRS:
            n = slot(direction, kind, 1, h)
            arrive(("sum", n), ring_recv.at[n])
            total = total + ring_recv[n].astype(jnp.float32)
        return total

    for h in (0, 1):
        last_send[h] = last_sum(KIND_O, h).astype(jnp.bfloat16)
        send(LAST, ("last", h), last_send.at[h], last_recv.at[h], to_side)
    for h in (0, 1):
        grad_out[pl.ds(h * quarter, quarter), :] = last_sum(KIND_A, h)
    for h in (0, 1):
        total = last_sum(KIND_B, h)
        arrive(("last", h), last_recv.at[h])
        grad_out[pl.ds(half + h * quarter, quarter), :] = total + last_recv[h].astype(
            jnp.float32
        )
    drain(RING, gathered.at[pl.ds(0, 21 * half), :])
    drain(SIDE, gathered.at[pl.ds(0, 9 * half), :])
    drain(CORE, gathered.at[pl.ds(0, 16 * rows), :])
    drain(CHIP, chip_send)
    drain(PAIR, pair_send)
    drain(SUM, ring_send.at[pl.ds(0, 42)])
    drain(LAST, last_send)
    if n_x > 1:
        drain(ACROSS_X, x_recv)
    if n_y > 1:
        drain(ACROSS_Y, y_recv)


def exchange(n_replica, inputs, doc_ids, values, cotangent, weights, local, current, moment, index):
    tokens, width = inputs.shape
    head = values.shape[1]
    rows = width // (4 * Z)
    half, quarter = rows // 2, rows // 4
    n_x = min(4, n_replica)
    n_y = n_replica // n_x
    bf16, f32 = jnp.bfloat16, jnp.float32
    anywhere = pl.BlockSpec(memory_space=pl.ANY)
    vmem = pl.BlockSpec(memory_space=pltpu.VMEM)
    return pl.pallas_call(
        functools.partial(kernel, n_x, n_y, Lanes()),
        out_shape=(
            jax.ShapeDtypeStruct((rows, 2 * head), f32),
            jax.ShapeDtypeStruct((width // 128, 128), f32),
            jax.ShapeDtypeStruct((width // 128, 128), f32),
        ),
        in_specs=[anywhere] * 9,
        out_specs=(vmem, vmem, vmem),
        scratch_shapes=[
            pltpu.SMEM((1,), jnp.int32),
            pltpu.VMEM((tokens, width), bf16),
            pltpu.VMEM((width, tokens), bf16),
            pltpu.VMEM((rows, 2 * head), f32),
            pltpu.VMEM((width, 2 * head), bf16),
            pltpu.VMEM((tokens, 2 * head), f32),
            pltpu.VMEM((1, tokens), jnp.int32),
            pltpu.VMEM((tokens, head), bf16),
            pltpu.VMEM((tokens, head), bf16),
            pltpu.VMEM((tokens, tokens), f32),
            pltpu.VMEM((tokens, tokens), f32),
            pltpu.VMEM((tokens, 2 * head), bf16),
            pltpu.VMEM(local.shape, bf16),
            pltpu.VMEM(current.shape, f32),
            pltpu.VMEM(moment.shape, f32),
            pltpu.VMEM((1, width), f32),
            pltpu.VMEM((max(n_x - 1, 1), 1, width), f32),
            pltpu.VMEM((1, width), f32),
            pltpu.VMEM((max(n_y - 1, 1), 1, width), f32),
            pltpu.VMEM((8, 2, rows, 2 * head), f32),
            pltpu.VMEM((8, 2, rows, 2 * head), bf16),
            pltpu.VMEM((8, 2, rows, 2 * head), bf16),
            pltpu.VMEM((8, half, 2 * head), bf16),
            pltpu.VMEM((8, half, 2 * head), bf16),
            pltpu.VMEM((48, quarter, 2 * head), bf16),
            pltpu.VMEM((48, quarter, 2 * head), bf16),
            pltpu.VMEM((2, quarter, 2 * head), bf16),
            pltpu.VMEM((2, quarter, 2 * head), bf16),
            pltpu.SemaphoreType.DMA((9,)),
            pltpu.SemaphoreType.DMA((9,)),
            pltpu.SemaphoreType.DMA((98,)),
        ],
        compiler_params=pltpu.CompilerParams(
            collective_id=0, has_side_effects=True, vmem_limit_bytes=56 * 1024 * 1024
        ),
    )(index, inputs, doc_ids, values, cotangent, weights, local, current, moment)


def on_device(
    n_replica,
    inputs,
    doc_ids,
    values,
    cotangent,
    weights,
    moment1,
    moment2,
    frag_local,
    frag_global,
    frag_moment,
    frag_index,
):
    gradient, new_global, new_moment = exchange(
        n_replica,
        inputs,
        doc_ids,
        values,
        cotangent,
        weights,
        frag_local[0, :, 0, :],
        frag_global,
        frag_moment,
        frag_index,
    )
    first_new = beta_one * moment1 + (1.0 - beta_one) * gradient
    second_new = beta_two * moment2 + (1.0 - beta_two) * gradient * gradient
    first_hat = first_new / (1.0 - beta_one**ADAM_STEP)
    second_hat = second_new / (1.0 - beta_two**ADAM_STEP)
    weight_new = weights - learn_rate * (
        first_hat / (jnp.sqrt(second_hat) + 1e-08) + decay_rate * weights
    )
    shape = (1, inputs.shape[1])
    return (
        weight_new,
        first_new,
        second_new,
        new_global.reshape(shape),
        new_moment.reshape(shape),
    )


def solution(mesh):
    both = P(("replica", "shard"), None)
    return jax.shard_map(
        functools.partial(on_device, mesh.shape["replica"]),
        mesh=mesh,
        in_specs=(both,) * 7
        + (
            P("replica", None, "shard", None),
            P(None, "shard", None),
            P(None, "shard", None),
            P(),
        ),
        out_specs=(both, both, both, P("shard", None), P("shard", None)),
        check_vma=False,
    )
```

```python
import functools
import math

import jax
import jax.numpy as jnp
from jax import lax
from jax.experimental import pallas as pl
from jax.experimental.pallas import tpu as pltpu
from jax.sharding import PartitionSpec as P

ADAM_STEP = 100

epsilon = 1e-06
beta_one = 0.9
beta_two = 0.95
learn_rate = 0.01
decay_rate = 0.1
outer_momentum = 0.9
outer_rate = 0.7

Z = 8
DIRS = (1, -1)
KIND_A, KIND_B, KIND_O = 0, 1, 2
RING, SIDE, CORE, CHIP, PAIR, SUM, LAST, ACROSS_X, ACROSS_Y = range(9)
ORDER = (4, 3, -3, 2, -2, 1, -1, 0)


class Lanes:
    def __init__(self):
        self.numbers = {}

    def __call__(self, *key):
        return self.numbers.setdefault(key, len(self.numbers))


def kernel(
    n_x,
    n_y,
    lanes,
    index_hbm,
    x_hbm,
    doc_hbm,
    val_hbm,
    cot_hbm,
    w_hbm,
    local_hbm,
    global_hbm,
    moment_hbm,
    grad_out,
    global_out,
    moment_out,
    index_buf,
    x_buf,
    xt_buf,
    w_buf,
    gathered,
    proj,
    doc_buf,
    val_buf,
    cot_buf,
    allowed_buf,
    grad_att,
    gp_buf,
    local_buf,
    global_buf,
    moment_buf,
    drift_buf,
    x_recv,
    xsum_buf,
    y_recv,
    sums,
    chip_send,
    chip_recv,
    pair_send,
    pair_recv,
    ring_send,
    ring_recv,
    last_send,
    last_recv,
    load_sem,
    send_sem,
    recv_sem,
    ready_sem,
):
    tokens, width = x_buf.shape
    head = val_buf.shape[1]
    rows = width // (4 * Z)
    half, quarter = rows // 2, rows // 4

    replica = lax.axis_index("replica")
    shard = lax.axis_index("shard")
    my_x, my_y = replica // n_y, lax.rem(replica, n_y)
    side, z, core = shard // 16, lax.rem(shard // 2, Z), lax.rem(shard, 2)
    other = 1 - side

    def at_z(step):
        return lax.rem(z + step + 2 * Z, Z)

    def unit(col, zz, cc):
        return col * 16 + zz * 2 + cc

    to_core = {"shard": unit(side, z, 1 - core)}
    to_side = {"shard": unit(other, z, core)}
    to_z = {d: {"shard": unit(side, at_z(d), core)} for d in DIRS}
    to_x = [{"replica": lax.rem(my_x + k, n_x) * n_y + my_y} for k in range(1, n_x)]
    to_y = [{"replica": my_x * n_y + lax.rem(my_y + k, n_y)} for k in range(1, n_y)]

    def describe(stream, key, src, dst, target):
        return pltpu.make_async_remote_copy(
            src_ref=src,
            dst_ref=dst,
            send_sem=send_sem.at[stream],
            recv_sem=recv_sem.at[lanes(*key)],
            device_id=target,
            device_id_type=pl.DeviceIdType.MESH,
        )

    def send(stream, key, src, dst, target):
        describe(stream, key, src, dst, target).start()

    def arrive(key, dst):
        describe(0, key, dst, dst, to_core).wait_recv()

    def drain(stream, src):
        describe(stream, ("core", 0), src, src, to_core).wait_send()

    barrier = pltpu.get_barrier_semaphore()

    def signal(sem, target):
        pl.semaphore_signal(
            sem, inc=1, device_id=target, device_id_type=pl.DeviceIdType.MESH
        )

    near = [(other, z), (side, at_z(1)), (side, at_z(-1))]
    far = [
        {"replica": target["replica"], "shard": unit(side, z, 1)} for target in to_x + to_y
    ]
    for col, zz in near:
        signal(barrier, {"shard": unit(col, zz, 0)})

    @pl.when(core == 1)
    def _():
        signal(barrier, to_core)

    for target in far:
        signal(barrier, target)

    def meet(count, counter, sem):
        @pl.when(core == counter)
        def _():
            pl.semaphore_wait(barrier, count)
            signal(sem, to_core)

        @pl.when(core != counter)
        def _():
            pl.semaphore_wait(sem, 1)

    def load(n, src, dst):
        copy = pltpu.make_async_copy(src, dst, load_sem.at[n])
        copy.start()
        return copy

    load_w = load(0, w_hbm, w_buf)
    load_local = load(1, local_hbm, local_buf)
    load_global = load(2, global_hbm, global_buf)
    load_x = load(3, x_hbm, x_buf)
    load_doc = load(4, doc_hbm, doc_buf)
    load_val = load(5, val_hbm, val_buf)
    load_cot = load(6, cot_hbm, cot_buf)
    load_moment = load(7, moment_hbm, moment_buf)
    load_index = load(8, index_hbm, index_buf)

    def span(col, zz, cc, lo, count):
        start = pl.multiple_of(unit(col, zz, cc) * rows + lo, 16)
        return gathered.at[pl.ds(start, count), :]

    load_w.wait()
    span(side, z, core, 0, rows)[...] = w_buf[...].astype(jnp.bfloat16)

    load_index.wait()
    chosen = index_buf[0]
    load_local.wait()
    load_global.wait()
    current = global_buf[chosen]
    local_rows = local_buf[...].astype(jnp.float32)
    picked = lax.broadcasted_iota(jnp.int32, local_rows.shape, 0) == chosen
    local_copy = jnp.sum(jnp.where(picked, local_rows, 0.0), axis=0, keepdims=True)
    drift_buf[...] = (current - local_copy).astype(jnp.bfloat16).astype(jnp.float32)

    meet(2 * len(near) + 1, 0, ready_sem.at[0])

    def piece(kind, direction, d, cc):
        zz = at_z(-direction * d)
        col = other if kind == KIND_O else side
        lo = 0 if kind == KIND_A else half
        if d == 4:
            return span(col, zz, cc, lo + (0 if direction == 1 else quarter), quarter)
        return span(col, zz, cc, lo, half)

    def side_piece(direction, d, cc, col):
        zz = at_z(-direction * d)
        if d == 4:
            return span(col, zz, cc, 0 if direction == 1 else quarter, quarter)
        return span(col, zz, cc, 0, half)

    def ring_on(kind, direction, d):
        if d < 4:
            src = piece(kind, direction, d, core)
            if d == 3:
                zz = at_z(-direction * d)
                col = other if kind == KIND_O else side
                lo = 0 if kind == KIND_A else half
                src = span(col, zz, core, lo + (0 if direction == 1 else quarter), quarter)
            send(RING, ("ring", kind, direction, d + 1), src, src, to_z[direction])

    def side_on(d, got):
        send(SIDE, ("side", d), got, got, to_side)

    def core_on(d, got):
        send(CORE, ("core", d), got, got, to_core)

    first_a = span(side, z, core, 0, half)
    first_b = span(side, z, core, half, half)
    their_b = span(other, z, core, half, half)
    for direction in DIRS:
        ring_on(KIND_A, direction, 0)
    send(SIDE, ("sideB",), first_b, first_b, to_side)
    for direction in DIRS:
        ring_on(KIND_B, direction, 0)
    side_on(0, first_a)
    core_on(0, span(side, z, core, 0, rows))

    load_x.wait()
    block = 2 * rows

    def transpose_block(p):
        cols = slice(p * block, (p + 1) * block)
        turned = x_buf[:, cols].T
        for cc in (0, 1):
            start = pl.multiple_of(p * block + (core if cc == 0 else 1 - core) * rows, 64)
            xt_buf[pl.ds(start, rows), :] = turned[cc * rows : (cc + 1) * rows]

    def make_allowed():
        load_doc.wait()
        by_column = jnp.broadcast_to(doc_buf[...], (tokens, tokens))
        by_row = by_column.T
        row = lax.broadcasted_iota(jnp.int32, (tokens, tokens), 0)
        column = lax.broadcasted_iota(jnp.int32, (tokens, tokens), 1)
        same = (by_row == by_column) & (column <= row)
        allowed_buf[...] = jnp.where(same, 1.0, 0.0)

    def make_grad_att():
        load_val.wait()
        load_cot.wait()
        grad_att[...] = lax.dot_general(
            cot_buf[...],
            val_buf[...],
            (((1,), (1,)), ((), ())),
            preferred_element_type=jnp.float32,
        )

    def multiply(col, zz, first=False):
        start = pl.multiple_of(unit(col, zz, 0) * rows, 128)
        term = jnp.dot(
            x_buf[:, pl.ds(start, block)],
            gathered[pl.ds(start, block), :],
            preferred_element_type=jnp.float32,
        )
        if first:
            proj[...] = term
        else:
            proj[...] += term

    def arrive_core(d):
        count = 2 * rows if d in (0, 4) else 4 * rows
        arrive(("core", d), gathered.at[pl.ds(0, count), :])

    fillers = [functools.partial(transpose_block, p) for p in range(2 * Z)]
    fillers += [make_allowed, make_grad_att]

    def fill(count=1):
        for _ in range(min(count, len(fillers))):
            fillers.pop(0)()

    def queue_products(d):
        fillers.append(functools.partial(arrive_core, d))
        for direction in DIRS if 0 < d < 4 else (1,):
            for col in (side, other):
                fillers.append(
                    functools.partial(
                        multiply, col, at_z(-direction * d), first=d == 0 and col is side
                    )
                )

    def sums_over_x():
        total = drift_buf[...]
        if n_x > 1:
            arrive(("x",), x_recv)
        for k in range(n_x - 1):
            total = total + x_recv[k]
        xsum_buf[...] = total
        for k, target in enumerate(to_y):
            send(ACROSS_Y, ("y",), xsum_buf, y_recv.at[k], target)

    def from_side(d):
        arrive(("side", d), gathered.at[pl.ds(0, half if d in (0, 4) else rows), :])
        for direction in DIRS if d else (1,):
            core_on(d, side_piece(direction, d, core, other))

    def from_ring(kind, d):
        for direction in DIRS:
            got = piece(kind, direction, d, core)
            arrive(("ring", kind, direction, d), got)
            ring_on(kind, direction, d)
            if kind == KIND_A:
                side_on(d, got)
            core_on(d, got)

    arrive(("sideB",), their_b)
    for direction in DIRS:
        ring_on(KIND_O, direction, 0)
    core_on(0, their_b)
    fill(4)
    for d in range(1, 5):
        from_ring(KIND_A, d)
        fill(2)
        from_side(d - 1)
        from_ring(KIND_B, d)
        fill(2)
        from_ring(KIND_O, d)
        if d == 2 and far:
            meet(2 * len(far), 1, ready_sem.at[1])
            for k, target in enumerate(to_x):
                send(ACROSS_X, ("x",), drift_buf, x_recv.at[k], target)
        fill(2)
        queue_products(d - 1)
    from_side(4)
    queue_products(4)
    fill(len(fillers))

    input_scale = 1.0 / math.sqrt(width)
    score_scale = 1.0 / math.sqrt(head)
    exact = lax.Precision.HIGHEST
    scaled = proj[...] * input_scale
    queries, keys_part = scaled[:, :head], scaled[:, head:]
    q_rate = lax.rsqrt(jnp.mean(queries * queries, axis=1, keepdims=True) + epsilon)
    k_rate = lax.rsqrt(jnp.mean(keys_part * keys_part, axis=1, keepdims=True) + epsilon)
    q_unit, k_unit = queries * q_rate, keys_part * k_rate
    scores = (
        lax.dot_general(
            q_unit,
            k_unit,
            (((1,), (1,)), ((), ())),
            precision=exact,
            preferred_element_type=jnp.float32,
        )
        * score_scale
    )
    raised = jnp.where(allowed_buf[...] > 0.5, jnp.exp(scores), 0.0)
    attention = raised / jnp.sum(raised, axis=1, keepdims=True)
    weighted = attention * grad_att[...]
    grad_scores = (
        weighted - attention * jnp.sum(weighted, axis=1, keepdims=True)
    ) * score_scale
    grad_qunit = jnp.dot(
        grad_scores, k_unit, precision=exact, preferred_element_type=jnp.float32
    )
    grad_kunit = jnp.dot(
        grad_scores.T, q_unit, precision=exact, preferred_element_type=jnp.float32
    )
    grad_query = q_rate * (
        grad_qunit - q_unit * jnp.mean(grad_qunit * q_unit, axis=1, keepdims=True)
    )
    grad_keys = k_rate * (
        grad_kunit - k_unit * jnp.mean(grad_kunit * k_unit, axis=1, keepdims=True)
    )
    gp_buf[:, :head] = (grad_query * input_scale).astype(jnp.bfloat16)
    gp_buf[:, head:] = (grad_keys * input_scale).astype(jnp.bfloat16)

    def place(delta):
        return ORDER.index(delta)

    def compute(delta):
        i, zz = place(delta), at_z(delta)
        for k, col in ((1, other), (0, side)):
            start = pl.multiple_of(unit(col, zz, 0) * rows, 128)
            term = jnp.dot(
                xt_buf[pl.ds(start, block), :],
                gp_buf[...],
                preferred_element_type=jnp.float32,
            )
            chip_send[i, k] = term[rows:].astype(jnp.bfloat16)
            sums[i, k] = term[:rows]
        send(CHIP, ("chip", i), chip_send.at[i], chip_recv.at[i], to_core)

    def pair(delta):
        i = place(delta)
        arrive(("chip", i), chip_recv.at[i])
        for k in (1, 0):
            sums[i, k] += chip_recv[i, k].astype(jnp.float32)
            if k == 1:
                pair_send[i] = sums[i, 1, :half].astype(jnp.bfloat16)
                send(PAIR, ("pair", i), pair_send.at[i], pair_recv.at[i], to_side)

    def across(delta):
        i = place(delta)
        arrive(("pair", i), pair_recv.at[i])
        sums[i, 0, :half] += pair_recv[i].astype(jnp.float32)

    def early(direction):
        return 1 if direction == 1 else 0

    def slot(direction, kind, d, h):
        return ((0 if direction == 1 else 1) * 3 + kind) * 8 + (d - 1) * 2 + h

    def ring_sum(kind, direction, d, h):
        delta = 4 if d == 4 else direction * d
        k = 1 if kind == KIND_O else 0
        lo = (0 if kind == KIND_A else half) + h * quarter
        total = sums[place(delta), k, lo : lo + quarter]
        if d < 3 or (d == 3 and h != early(direction)):
            n = slot(direction, kind, d + 1, h)
            arrive(("sum", n), ring_recv.at[n])
            total = total + ring_recv[n].astype(jnp.float32)
        n = slot(direction, kind, d, h)
        ring_send[n] = total.astype(jnp.bfloat16)
        send(SUM, ("sum", n), ring_send.at[n], ring_recv.at[n], to_z[direction])

    def sum_on(kinds, d, first, directions=DIRS):
        for kind in kinds:
            for direction in directions:
                h = early(direction) if first else 1 - early(direction)
                ring_sum(kind, direction, d, h)

    whole, split = (KIND_O, KIND_B), (KIND_A,)
    compute(4)
    compute(3)
    sums_over_x()
    pair(4)
    sum_on(whole, 4, False)
    compute(-3)
    pair(3)
    sum_on(whole, 3, True, (1,))
    compute(2)
    pair(-3)
    sum_on(whole, 3, True, (-1,))
    compute(-2)
    pair(2)
    compute(1)
    pair(-2)
    across(4)
    sum_on(split, 4, False)
    sum_on(whole, 3, False)
    compute(-1)
    pair(1)
    sum_on(whole, 2, True)
    compute(0)
    pair(-1)
    across(3)
    across(-3)
    sum_on(split, 3, True)
    sum_on(split, 3, False)
    pair(0)
    sum_on(whole, 2, False)
    sum_on(whole, 1, True)
    across(2)
    across(-2)
    sum_on(split, 2, True)
    sum_on(split, 2, False)
    sum_on(whole, 1, False)
    across(1)
    across(-1)
    sum_on(split, 1, True)
    sum_on(split, 1, False)

    load_moment.wait()
    total = xsum_buf[...]
    if n_y > 1:
        arrive(("y",), y_recv)
    for k in range(n_y - 1):
        total = total + y_recv[k]
    drift_mean = total / (n_x * n_y)
    new_moment = outer_momentum * moment_buf[chosen] + drift_mean
    new_global = global_buf[chosen] - outer_rate * (
        drift_mean + outer_momentum * new_moment
    )
    moment_out[...] = new_moment
    global_out[...] = new_global

    across(0)

    def last_sum(kind, h):
        k = 1 if kind == KIND_O else 0
        lo = (0 if kind == KIND_A else half) + h * quarter
        total = sums[place(0), k, lo : lo + quarter]
        for direction in DIRS:
            n = slot(direction, kind, 1, h)
            arrive(("sum", n), ring_recv.at[n])
            total = total + ring_recv[n].astype(jnp.float32)
        return total

    for h in (0, 1):
        last_send[h] = last_sum(KIND_O, h).astype(jnp.bfloat16)
        send(LAST, ("last", h), last_send.at[h], last_recv.at[h], to_side)
    for h in (0, 1):
        grad_out[pl.ds(h * quarter, quarter), :] = last_sum(KIND_A, h)
    for h in (0, 1):
        total = last_sum(KIND_B, h)
        arrive(("last", h), last_recv.at[h])
        grad_out[pl.ds(half + h * quarter, quarter), :] = total + last_recv[h].astype(
            jnp.float32
        )
    drain(RING, gathered.at[pl.ds(0, 21 * half), :])
    drain(SIDE, gathered.at[pl.ds(0, 9 * half), :])
    drain(CORE, gathered.at[pl.ds(0, 16 * rows), :])
    drain(CHIP, chip_send)
    drain(PAIR, pair_send)
    drain(SUM, ring_send.at[pl.ds(0, 42)])
    drain(LAST, last_send)
    if n_x > 1:
        drain(ACROSS_X, x_recv)
    if n_y > 1:
        drain(ACROSS_Y, y_recv)


def exchange(n_replica, inputs, doc_ids, values, cotangent, weights, local, current, moment, index):
    tokens, width = inputs.shape
    head = values.shape[1]
    rows = width // (4 * Z)
    half, quarter = rows // 2, rows // 4
    n_x = min(4, n_replica)
    n_y = n_replica // n_x
    bf16, f32 = jnp.bfloat16, jnp.float32
    anywhere = pl.BlockSpec(memory_space=pl.ANY)
    vmem = pl.BlockSpec(memory_space=pltpu.VMEM)
    return pl.pallas_call(
        functools.partial(kernel, n_x, n_y, Lanes()),
        out_shape=(
            jax.ShapeDtypeStruct((rows, 2 * head), f32),
            jax.ShapeDtypeStruct((1, width), f32),
            jax.ShapeDtypeStruct((1, width), f32),
        ),
        in_specs=[pl.BlockSpec(memory_space=pltpu.HBM)] + [anywhere] * 8,
        out_specs=(vmem, vmem, vmem),
        scratch_shapes=[
            pltpu.SMEM((1,), jnp.int32),
            pltpu.VMEM((tokens, width), bf16),
            pltpu.VMEM((width, tokens), bf16),
            pltpu.VMEM((rows, 2 * head), f32),
            pltpu.VMEM((width, 2 * head), bf16),
            pltpu.VMEM((tokens, 2 * head), f32),
            pltpu.VMEM((1, tokens), jnp.int32),
            pltpu.VMEM((tokens, head), bf16),
            pltpu.VMEM((tokens, head), bf16),
            pltpu.VMEM((tokens, tokens), f32),
            pltpu.VMEM((tokens, tokens), f32),
            pltpu.VMEM((tokens, 2 * head), bf16),
            pltpu.VMEM(local.shape, bf16),
            pltpu.VMEM(current.shape, f32),
            pltpu.VMEM(moment.shape, f32),
            pltpu.VMEM((1, width), f32),
            pltpu.VMEM((max(n_x - 1, 1), 1, width), f32),
            pltpu.VMEM((1, width), f32),
            pltpu.VMEM((max(n_y - 1, 1), 1, width), f32),
            pltpu.VMEM((8, 2, rows, 2 * head), f32),
            pltpu.VMEM((8, 2, rows, 2 * head), bf16),
            pltpu.VMEM((8, 2, rows, 2 * head), bf16),
            pltpu.VMEM((8, half, 2 * head), bf16),
            pltpu.VMEM((8, half, 2 * head), bf16),
            pltpu.VMEM((48, quarter, 2 * head), bf16),
            pltpu.VMEM((48, quarter, 2 * head), bf16),
            pltpu.VMEM((2, quarter, 2 * head), bf16),
            pltpu.VMEM((2, quarter, 2 * head), bf16),
            pltpu.SemaphoreType.DMA((9,)),
            pltpu.SemaphoreType.DMA((9,)),
            pltpu.SemaphoreType.DMA((98,)),
            pltpu.SemaphoreType.REGULAR((2,)),
        ],
        compiler_params=pltpu.CompilerParams(
            collective_id=0, has_side_effects=True, vmem_limit_bytes=56 * 1024 * 1024
        ),
    )(index, inputs, doc_ids, values, cotangent, weights, local, current, moment)


def finish(
    grad, weights, moment1, moment2, new_global, new_moment, out_w, out_1, out_2, out_g, out_m
):
    gradient, rows = grad[...], weights[...]
    first_new = beta_one * moment1[...] + (1.0 - beta_one) * gradient
    second_new = beta_two * moment2[...] + (1.0 - beta_two) * gradient * gradient
    first_hat = first_new / (1.0 - beta_one**ADAM_STEP)
    second_hat = second_new / (1.0 - beta_two**ADAM_STEP)
    out_w[...] = rows - learn_rate * (
        first_hat / (jnp.sqrt(second_hat) + 1e-08) + decay_rate * rows
    )
    out_1[...] = first_new
    out_2[...] = second_new
    out_g[...] = new_global[...]
    out_m[...] = new_moment[...]


def on_device(
    n_replica,
    inputs,
    doc_ids,
    values,
    cotangent,
    weights,
    moment1,
    moment2,
    frag_local,
    frag_global,
    frag_moment,
    frag_index,
):
    gradient, new_global, new_moment = exchange(
        n_replica,
        inputs,
        doc_ids,
        values,
        cotangent,
        weights,
        frag_local[0, :, 0, :],
        frag_global,
        frag_moment,
        frag_index,
    )
    vmem = pl.BlockSpec(memory_space=pltpu.VMEM)
    like = jax.ShapeDtypeStruct(weights.shape, jnp.float32)
    row = jax.ShapeDtypeStruct(new_global.shape, jnp.float32)
    return pl.pallas_call(
        finish,
        out_shape=(like, like, like, row, row),
        in_specs=[vmem] * 6,
        out_specs=(vmem,) * 5,
    )(gradient, weights, moment1, moment2, new_global, new_moment)


def solution(mesh):
    both = P(("replica", "shard"), None)
    return jax.shard_map(
        functools.partial(on_device, mesh.shape["replica"]),
        mesh=mesh,
        in_specs=(both,) * 7
        + (
            P("replica", None, "shard", None),
            P(None, "shard", None),
            P(None, "shard", None),
            P(),
        ),
        out_specs=(both, both, both, P("shard", None), P("shard", None)),
        check_vma=False,
    )
```

```python
import functools
import math

import jax
import jax.numpy as jnp
from jax import lax
from jax.experimental import pallas as pl
from jax.experimental.pallas import tpu as pltpu
from jax.sharding import PartitionSpec as P

ADAM_STEP = 100

epsilon = 1e-06
beta_one = 0.9
beta_two = 0.95
learn_rate = 0.01
decay_rate = 0.1
outer_momentum = 0.9
outer_rate = 0.7

Z = 8
WAYS = ((1, 0), (-1, 1))
KIND_A, KIND_B, KIND_O = 0, 1, 2
RING, SIDE, CORE, CHIP, PAIR, SUM, LAST, ACROSS_X, ACROSS_Y = range(9)
ORDER = (4, 3, -3, 2, -2, 1, -1, 0)


class Lanes:
    def __init__(self):
        self.numbers = {}
        self.count = 0

    def __call__(self, *key, width=1):
        if key not in self.numbers:
            self.numbers[key] = self.count
            self.count += width
        return self.numbers[key]


def kernel(
    n_x,
    n_y,
    lanes,
    index_hbm,
    x_hbm,
    doc_hbm,
    val_hbm,
    cot_hbm,
    w_hbm,
    local_hbm,
    global_hbm,
    moment_hbm,
    grad_out,
    global_out,
    moment_out,
    index_buf,
    x_buf,
    xt_buf,
    w_buf,
    gathered,
    proj,
    doc_buf,
    val_buf,
    cot_buf,
    allowed_buf,
    grad_att,
    gp_buf,
    local_buf,
    global_buf,
    moment_buf,
    drift_buf,
    x_recv,
    xsum_buf,
    y_recv,
    sums,
    chip_send,
    chip_recv,
    pair_send,
    pair_recv,
    ring_send,
    ring_recv,
    last_send,
    last_recv,
    load_sem,
    send_sem,
    recv_sem,
    ready_sem,
):
    tokens, width = x_buf.shape
    head = val_buf.shape[1]
    rows = width // (4 * Z)
    half, quarter = rows // 2, rows // 4

    replica = lax.axis_index("replica")
    shard = lax.axis_index("shard")
    my_x, my_y = replica // n_y, lax.rem(replica, n_y)
    side, z, core = shard // 16, lax.rem(shard // 2, Z), lax.rem(shard, 2)
    other = 1 - side

    def at_z(step):
        return lax.rem(z + step + 2 * Z, Z)

    def unit(col, zz, cc):
        return col * 16 + zz * 2 + cc

    to_core = {"shard": unit(side, z, 1 - core)}
    to_side = {"shard": unit(other, z, core)}

    def to_z(way):
        return {"shard": unit(side, at_z(way[0]), core)}

    bit = jnp.where(z == 0, 1, 0)
    ways = ((1 - 2 * bit, bit), (2 * bit - 1, 1 - bit))
    to_x = [{"replica": lax.rem(my_x + k, n_x) * n_y + my_y} for k in range(1, n_x)]
    to_y = [{"replica": my_x * n_y + lax.rem(my_y + k, n_y)} for k in range(1, n_y)]

    def describe(stream, key, src, dst, target):
        return pltpu.make_async_remote_copy(
            src_ref=src,
            dst_ref=dst,
            send_sem=send_sem.at[stream],
            recv_sem=recv_sem.at[key if not isinstance(key, tuple) else lanes(*key)],
            device_id=target,
            device_id_type=pl.DeviceIdType.MESH,
        )

    def send(stream, key, src, dst, target):
        describe(stream, key, src, dst, target).start()

    def arrive(key, dst):
        describe(0, key, dst, dst, to_core).wait_recv()

    def drain(stream, src):
        describe(stream, ("mine", 0), src, src, to_core).wait_send()

    barrier = pltpu.get_barrier_semaphore()

    def signal(sem, target):
        pl.semaphore_signal(
            sem, inc=1, device_id=target, device_id_type=pl.DeviceIdType.MESH
        )

    near = [(other, z), (side, at_z(1)), (side, at_z(-1))]
    far = [
        {"replica": target["replica"], "shard": unit(side, z, 1)} for target in to_x + to_y
    ]
    for col, zz in near:
        signal(barrier, {"shard": unit(col, zz, 0)})

    @pl.when(core == 1)
    def _():
        signal(barrier, to_core)

    for target in far:
        signal(barrier, target)

    def meet(count, counter, sem):
        @pl.when(core == counter)
        def _():
            pl.semaphore_wait(barrier, count)
            signal(sem, to_core)

        @pl.when(core != counter)
        def _():
            pl.semaphore_wait(sem, 1)

    def load(n, src, dst):
        copy = pltpu.make_async_copy(src, dst, load_sem.at[n])
        copy.start()
        return copy

    load_w = load(0, w_hbm, w_buf)
    load_local = load(1, local_hbm, local_buf)
    load_global = load(2, global_hbm, global_buf)
    load_doc = load(4, doc_hbm, doc_buf)
    load_val = load(5, val_hbm, val_buf)
    load_cot = load(6, cot_hbm, cot_buf)
    load_moment = load(7, moment_hbm, moment_buf)
    load_index = load(8, index_hbm, index_buf)

    def span(col, zz, cc, lo, count):
        start = pl.multiple_of(unit(col, zz, cc) * rows + lo, 16)
        return gathered.at[pl.ds(start, count), :]

    load_w.wait()
    span(side, z, core, 0, rows)[...] = w_buf[...].astype(jnp.bfloat16)

    meet(2 * len(near) + 1, 0, ready_sem.at[0])

    def piece(kind, way, d, cc, h):
        zz = at_z(-way[0] * d)
        col = other if kind == KIND_O else side
        lo = 0 if kind == KIND_A else half
        if h is None:
            return span(col, zz, cc, lo, half)
        return span(col, zz, cc, lo + h * quarter, quarter)

    def part(way, q):
        return None if q is None else way[1] if q == 0 else 1 - way[1]

    def side_piece(way, d, cc, col):
        zz = at_z(-way[0] * d)
        if d == 4:
            return span(col, zz, cc, part(way, 0) * quarter, quarter)
        return span(col, zz, cc, 0, half)

    def ring_lane(kind, way, d, q):
        if kind == KIND_B:
            return lanes("ring", kind, d, width=2) + way[1]
        if d == 4:
            return lanes("ring", kind, d, width=2) + way[1]
        return lanes("ring", kind, d, width=4) + 2 * q + way[1]

    def ring_on(kind, way, d, q):
        if d == 3 and q is None:
            q = 0
        if d < 3 or (d == 3 and q == 0):
            src = piece(kind, way, d, core, part(way, q))
            send(RING, ring_lane(kind, way, d + 1, q), src, src, to_z(way))

    def side_on(d, got):
        send(SIDE, ("side", d), got, got, to_side)

    def core_on(name, d, got):
        send(CORE, (name, d), got, got, to_core)

    first_a = span(side, z, core, 0, half)
    for h in (0, 1):
        first_b = span(side, z, core, half + h * quarter, quarter)
        send(SIDE, ("sideB", h), first_b, first_b, to_side)
    for q in (0, 1):
        for way in WAYS:
            ring_on(KIND_A, way, 0, q)
    for way in WAYS:
        ring_on(KIND_B, way, 0, None)
    load_x = load(3, x_hbm, x_buf)

    block = 2 * rows

    def make_drift():
        load_index.wait()
        load_local.wait()
        load_global.wait()
        chosen = index_buf[0]
        current = global_buf[chosen]
        local_rows = local_buf[...].astype(jnp.float32)
        picked = lax.broadcasted_iota(jnp.int32, local_rows.shape, 0) == chosen
        local_copy = jnp.sum(jnp.where(picked, local_rows, 0.0), axis=0, keepdims=True)
        drift_buf[...] = (current - local_copy).astype(jnp.bfloat16).astype(jnp.float32)

    def transpose_block(p):
        cols = slice(p * block, (p + 1) * block)
        turned = x_buf[:, cols].T
        for cc in (0, 1):
            start = pl.multiple_of(p * block + (core if cc == 0 else 1 - core) * rows, 64)
            xt_buf[pl.ds(start, rows), :] = turned[cc * rows : (cc + 1) * rows]

    def make_allowed():
        load_doc.wait()
        by_column = jnp.broadcast_to(doc_buf[...], (tokens, tokens))
        by_row = by_column.T
        row = lax.broadcasted_iota(jnp.int32, (tokens, tokens), 0)
        column = lax.broadcasted_iota(jnp.int32, (tokens, tokens), 1)
        same = (by_row == by_column) & (column <= row)
        allowed_buf[...] = jnp.where(same, 1.0, 0.0)

    def make_grad_att():
        load_val.wait()
        load_cot.wait()
        grad_att[...] = lax.dot_general(
            cot_buf[...],
            val_buf[...],
            (((1,), (1,)), ((), ())),
            preferred_element_type=jnp.float32,
        )

    def multiply(col, zz, first=False):
        start = pl.multiple_of(unit(col, zz, 0) * rows, 128)
        term = jnp.dot(
            x_buf[:, pl.ds(start, block)],
            gathered[pl.ds(start, block), :],
            preferred_element_type=jnp.float32,
        )
        if first:
            proj[...] = term
        else:
            proj[...] += term

    def arrive_core(name, d):
        count = rows if d in (0, 4) else 2 * rows
        arrive((name, d), gathered.at[pl.ds(0, count), :])

    fillers = [make_drift, make_allowed, make_grad_att, load_x.wait]
    fillers += [functools.partial(transpose_block, p) for p in range(2 * Z)]

    def fill(count=1):
        for _ in range(min(count, len(fillers))):
            fillers.pop(0)()

    def queue_products(name, d):
        col = side if name == "mine" else other
        fillers.append(functools.partial(arrive_core, name, d))
        for step, _ in WAYS if 0 < d < 4 else WAYS[:1]:
            fillers.append(
                functools.partial(
                    multiply, col, at_z(-step * d), first=d == 0 and name == "mine"
                )
            )

    def sums_over_x():
        total = drift_buf[...]
        if n_x > 1:
            arrive(("x",), x_recv)
        for k in range(n_x - 1):
            total = total + x_recv[k]
        xsum_buf[...] = total
        for k, target in enumerate(to_y):
            send(ACROSS_Y, ("y",), xsum_buf, y_recv.at[k], target)

    def from_side(d):
        arrive(("side", d), gathered.at[pl.ds(0, half if d in (0, 4) else rows), :])
        for way in WAYS if d else WAYS[:1]:
            core_on("theirs", d, side_piece(way, d, core, other))

    def from_ring(kind, d, q):
        for way in ways:
            got = piece(kind, way, d, core, part(way, 0 if d == 4 else q))
            arrive(ring_lane(kind, way, d, q), got)
            ring_on(kind, way, d, q)
            if kind == KIND_A:
                side_on(d, got)
            core_on("theirs" if kind == KIND_O else "mine", d, got)

    fill(3)
    for d in range(1, 5):
        for h in (0, 1):
            if d < 4 or h == 0:
                from_ring(KIND_A, d, h)
            if d == 1:
                their_b = span(other, z, core, half + h * quarter, quarter)
                arrive(("sideB", h), their_b)
                for way in WAYS:
                    ring_on(KIND_O, way, 0, h if way[1] == 0 else 1 - h)
                core_on("theirs", 0, their_b)
            else:
                from_ring(KIND_O, d - 1, h)
        if d == 1:
            side_on(0, first_a)
            core_on("mine", 0, span(side, z, core, 0, rows))
            queue_products("mine", 0)
        fill(3)
        from_ring(KIND_B, d, None)
        queue_products("mine", d)
        if d == 2 and far:
            meet(2 * len(far), 1, ready_sem.at[1])
            for k, target in enumerate(to_x):
                send(ACROSS_X, ("x",), drift_buf, x_recv.at[k], target)
        if d >= 2:
            from_side(d - 2)
            queue_products("theirs", d - 2)
        fill(5)
    from_side(3)
    queue_products("theirs", 3)
    fill(len(fillers) - 3)
    from_ring(KIND_O, 4, None)
    from_side(4)
    queue_products("theirs", 4)
    fill(len(fillers))
    sums_over_x()

    input_scale = 1.0 / math.sqrt(width)
    score_scale = 1.0 / math.sqrt(head)
    exact = lax.Precision.HIGHEST
    scaled = proj[...] * input_scale
    queries, keys_part = scaled[:, :head], scaled[:, head:]
    q_rate = lax.rsqrt(jnp.mean(queries * queries, axis=1, keepdims=True) + epsilon)
    k_rate = lax.rsqrt(jnp.mean(keys_part * keys_part, axis=1, keepdims=True) + epsilon)
    q_unit, k_unit = queries * q_rate, keys_part * k_rate
    scores = (
        lax.dot_general(
            q_unit,
            k_unit,
            (((1,), (1,)), ((), ())),
            precision=exact,
            preferred_element_type=jnp.float32,
        )
        * score_scale
    )
    raised = jnp.where(allowed_buf[...] > 0.5, jnp.exp(scores), 0.0)
    attention = raised / jnp.sum(raised, axis=1, keepdims=True)
    weighted = attention * grad_att[...]
    grad_scores = (
        weighted - attention * jnp.sum(weighted, axis=1, keepdims=True)
    ) * score_scale
    grad_qunit = jnp.dot(
        grad_scores, k_unit, precision=exact, preferred_element_type=jnp.float32
    )
    grad_kunit = jnp.dot(
        grad_scores.T, q_unit, precision=exact, preferred_element_type=jnp.float32
    )
    grad_query = q_rate * (
        grad_qunit - q_unit * jnp.mean(grad_qunit * q_unit, axis=1, keepdims=True)
    )
    grad_keys = k_rate * (
        grad_kunit - k_unit * jnp.mean(grad_kunit * k_unit, axis=1, keepdims=True)
    )
    gp_buf[:, :head] = (grad_query * input_scale).astype(jnp.bfloat16)
    gp_buf[:, head:] = (grad_keys * input_scale).astype(jnp.bfloat16)

    def place(delta):
        return ORDER.index(delta)

    def compute(delta):
        i, zz = place(delta), at_z(delta)
        for k, col in ((1, other), (0, side)):
            start = pl.multiple_of(unit(col, zz, 0) * rows, 128)
            term = jnp.dot(
                xt_buf[pl.ds(start, block), :],
                gp_buf[...],
                preferred_element_type=jnp.float32,
            )
            chip_send[i, k] = term[rows:].astype(jnp.bfloat16)
            sums[i, k] = term[:rows]
        send(CHIP, ("chip", i), chip_send.at[i], chip_recv.at[i], to_core)

    def pair(delta):
        i = place(delta)
        arrive(("chip", i), chip_recv.at[i])
        for k in (1, 0):
            sums[i, k] += chip_recv[i, k].astype(jnp.float32)
            if k == 1:
                pair_send[i] = sums[i, 1, :half].astype(jnp.bfloat16)
                send(PAIR, ("pair", i), pair_send.at[i], pair_recv.at[i], to_side)

    def across(delta):
        i = place(delta)
        arrive(("pair", i), pair_recv.at[i])
        sums[i, 0, :half] += pair_recv[i].astype(jnp.float32)

    def slot(way, kind, d, late):
        return way[1] * 24 + kind * 8 + (d - 1) * 2 + late

    first_sum = lanes("sum", width=48)

    def ring_sum(kind, way, d, late):
        i = 0 if d == 4 else 1 + 2 * (3 - d) + way[1]
        k = 1 if kind == KIND_O else 0
        h = way[1] if late else 1 - way[1]
        lo = (0 if kind == KIND_A else half) + h * quarter
        total = sums[i, k, pl.ds(pl.multiple_of(lo, 8), quarter)]
        if d < 3 or (d == 3 and late):
            n = slot(way, kind, d + 1, late)
            arrive(first_sum + n, ring_recv.at[n])
            total = total + ring_recv[n].astype(jnp.float32)
        n = slot(way, kind, d, late)
        ring_send[n] = total.astype(jnp.bfloat16)
        send(SUM, first_sum + n, ring_send.at[n], ring_recv.at[n], to_z(way))

    def sum_on(kinds, d, first, among=ways):
        for kind in kinds:
            for way in among:
                ring_sum(kind, way, d, 0 if first else 1)

    whole, split = (KIND_O, KIND_B), (KIND_A,)
    compute(4)
    compute(3)
    compute(-3)
    pair(4)
    sum_on(whole, 4, False)
    compute(2)
    pair(3)
    sum_on(whole, 3, True, WAYS[:1])
    compute(-2)
    pair(-3)
    sum_on(whole, 3, True, WAYS[1:])
    compute(1)
    pair(2)
    compute(-1)
    pair(-2)
    sum_on(whole, 3, False)
    compute(0)
    pair(1)
    across(4)
    sum_on(split, 4, False)
    sum_on(whole, 2, True)
    pair(-1)
    sum_on(whole, 2, False)
    across(3)
    across(-3)
    pair(0)
    sum_on(split, 3, False)
    sum_on(split, 3, True)
    sum_on(whole, 1, True)
    sum_on(whole, 1, False)
    across(2)
    across(-2)
    sum_on(split, 2, False)
    sum_on(split, 2, True)
    across(1)
    across(-1)

    def last_sum(kind, h):
        k = 1 if kind == KIND_O else 0
        lo = (0 if kind == KIND_A else half) + h * quarter
        total = sums[place(0), k, lo : lo + quarter]
        for way in WAYS:
            n = slot(way, kind, 1, 1 if h == way[1] else 0)
            arrive(first_sum + n, ring_recv.at[n])
            total = total + ring_recv[n].astype(jnp.float32)
        return total

    for h in (0, 1):
        last_send[h] = last_sum(KIND_O, h).astype(jnp.bfloat16)
        send(LAST, ("last", h), last_send.at[h], last_recv.at[h], to_side)
    sum_on(split, 1, False)
    sum_on(split, 1, True)
    across(0)

    load_moment.wait()
    chosen = index_buf[0]
    total = xsum_buf[...]
    if n_y > 1:
        arrive(("y",), y_recv)
    for k in range(n_y - 1):
        total = total + y_recv[k]
    drift_mean = total / (n_x * n_y)
    new_moment = outer_momentum * moment_buf[chosen] + drift_mean
    new_global = global_buf[chosen] - outer_rate * (
        drift_mean + outer_momentum * new_moment
    )
    moment_out[...] = new_moment
    global_out[...] = new_global

    for h in (0, 1):
        grad_out[pl.ds(h * quarter, quarter), :] = last_sum(KIND_A, h)
    for h in (0, 1):
        total = last_sum(KIND_B, h)
        arrive(("last", h), last_recv.at[h])
        grad_out[pl.ds(half + h * quarter, quarter), :] = total + last_recv[h].astype(
            jnp.float32
        )
    drain(RING, gathered.at[pl.ds(0, 21 * half), :])
    drain(SIDE, gathered.at[pl.ds(0, 9 * half), :])
    drain(CORE, gathered.at[pl.ds(0, 16 * rows), :])
    drain(CHIP, chip_send)
    drain(PAIR, pair_send)
    drain(SUM, ring_send.at[pl.ds(0, 42)])
    drain(LAST, last_send)
    if n_x > 1:
        drain(ACROSS_X, x_recv)
    if n_y > 1:
        drain(ACROSS_Y, y_recv)


def exchange(n_replica, inputs, doc_ids, values, cotangent, weights, local, current, moment, index):
    tokens, width = inputs.shape
    head = values.shape[1]
    rows = width // (4 * Z)
    half, quarter = rows // 2, rows // 4
    n_x = min(4, n_replica)
    n_y = n_replica // n_x
    bf16, f32 = jnp.bfloat16, jnp.float32
    anywhere = pl.BlockSpec(memory_space=pl.ANY)
    vmem = pl.BlockSpec(memory_space=pltpu.VMEM)
    return pl.pallas_call(
        functools.partial(kernel, n_x, n_y, Lanes()),
        out_shape=(
            jax.ShapeDtypeStruct((rows, 2 * head), f32),
            jax.ShapeDtypeStruct((1, width), f32),
            jax.ShapeDtypeStruct((1, width), f32),
        ),
        in_specs=[pl.BlockSpec(memory_space=pltpu.HBM)] + [anywhere] * 8,
        out_specs=(vmem, vmem, vmem),
        scratch_shapes=[
            pltpu.SMEM((1,), jnp.int32),
            pltpu.VMEM((tokens, width), bf16),
            pltpu.VMEM((width, tokens), bf16),
            pltpu.VMEM((rows, 2 * head), f32),
            pltpu.VMEM((width, 2 * head), bf16),
            pltpu.VMEM((tokens, 2 * head), f32),
            pltpu.VMEM((1, tokens), jnp.int32),
            pltpu.VMEM((tokens, head), bf16),
            pltpu.VMEM((tokens, head), bf16),
            pltpu.VMEM((tokens, tokens), f32),
            pltpu.VMEM((tokens, tokens), f32),
            pltpu.VMEM((tokens, 2 * head), bf16),
            pltpu.VMEM(local.shape, bf16),
            pltpu.VMEM(current.shape, f32),
            pltpu.VMEM(moment.shape, f32),
            pltpu.VMEM((1, width), f32),
            pltpu.VMEM((max(n_x - 1, 1), 1, width), f32),
            pltpu.VMEM((1, width), f32),
            pltpu.VMEM((max(n_y - 1, 1), 1, width), f32),
            pltpu.VMEM((8, 2, rows, 2 * head), f32),
            pltpu.VMEM((8, 2, rows, 2 * head), bf16),
            pltpu.VMEM((8, 2, rows, 2 * head), bf16),
            pltpu.VMEM((8, half, 2 * head), bf16),
            pltpu.VMEM((8, half, 2 * head), bf16),
            pltpu.VMEM((48, quarter, 2 * head), bf16),
            pltpu.VMEM((48, quarter, 2 * head), bf16),
            pltpu.VMEM((2, quarter, 2 * head), bf16),
            pltpu.VMEM((2, quarter, 2 * head), bf16),
            pltpu.SemaphoreType.DMA((9,)),
            pltpu.SemaphoreType.DMA((9,)),
            pltpu.SemaphoreType.DMA((124,)),
            pltpu.SemaphoreType.REGULAR((2,)),
        ],
        compiler_params=pltpu.CompilerParams(
            collective_id=0, has_side_effects=True, vmem_limit_bytes=56 * 1024 * 1024
        ),
    )(index, inputs, doc_ids, values, cotangent, weights, local, current, moment)


def finish(
    grad, weights, moment1, moment2, new_global, new_moment, out_w, out_1, out_2, out_g, out_m
):
    gradient, rows = grad[...], weights[...]
    first_new = beta_one * moment1[...] + (1.0 - beta_one) * gradient
    second_new = beta_two * moment2[...] + (1.0 - beta_two) * gradient * gradient
    first_hat = first_new / (1.0 - beta_one**ADAM_STEP)
    second_hat = second_new / (1.0 - beta_two**ADAM_STEP)
    out_w[...] = rows - learn_rate * (
        first_hat / (jnp.sqrt(second_hat) + 1e-08) + decay_rate * rows
    )
    out_1[...] = first_new
    out_2[...] = second_new
    out_g[...] = new_global[...]
    out_m[...] = new_moment[...]


def on_device(
    n_replica,
    inputs,
    doc_ids,
    values,
    cotangent,
    weights,
    moment1,
    moment2,
    frag_local,
    frag_global,
    frag_moment,
    frag_index,
):
    gradient, new_global, new_moment = exchange(
        n_replica,
        inputs,
        doc_ids,
        values,
        cotangent,
        weights,
        frag_local[0, :, 0, :],
        frag_global,
        frag_moment,
        frag_index,
    )
    vmem = pl.BlockSpec(memory_space=pltpu.VMEM)
    like = jax.ShapeDtypeStruct(weights.shape, jnp.float32)
    row = jax.ShapeDtypeStruct(new_global.shape, jnp.float32)
    return pl.pallas_call(
        finish,
        out_shape=(like, like, like, row, row),
        in_specs=[vmem] * 6,
        out_specs=(vmem,) * 5,
    )(gradient, weights, moment1, moment2, new_global, new_moment)


def solution(mesh):
    both = P(("replica", "shard"), None)
    return jax.shard_map(
        functools.partial(on_device, mesh.shape["replica"]),
        mesh=mesh,
        in_specs=(both,) * 7
        + (
            P("replica", None, "shard", None),
            P(None, "shard", None),
            P(None, "shard", None),
            P(),
        ),
        out_specs=(both, both, both, P("shard", None), P("shard", None)),
        check_vma=False,
    )
```

```python
import functools
import math

import jax
import jax.numpy as jnp
from jax import lax
from jax.experimental import pallas as pl
from jax.experimental.pallas import tpu as pltpu
from jax.sharding import PartitionSpec as P

ADAM_STEP = 100

epsilon = 1e-06
beta_one = 0.9
beta_two = 0.95
learn_rate = 0.01
decay_rate = 0.1
outer_momentum = 0.9
outer_rate = 0.7

Z = 8
WAYS = ((1, 0), (-1, 1))
KIND_A, KIND_B, KIND_O = 0, 1, 2
RING, SIDE, CORE, CHIP, PAIR, SUM, LAST, ACROSS_X, ACROSS_Y = range(9)
ORDER = (4, 3, -3, 2, -2, 1, -1, 0)


class Lanes:
    def __init__(self):
        self.numbers = {}
        self.count = 0

    def __call__(self, *key, width=1):
        if key not in self.numbers:
            self.numbers[key] = self.count
            self.count += width
        return self.numbers[key]


def kernel(
    n_x,
    n_y,
    lanes,
    index_hbm,
    x_hbm,
    doc_hbm,
    val_hbm,
    cot_hbm,
    w_hbm,
    local_hbm,
    global_hbm,
    moment_hbm,
    grad_out,
    global_out,
    moment_out,
    index_buf,
    x_buf,
    xt_buf,
    w_buf,
    gathered,
    proj,
    doc_buf,
    val_buf,
    cot_buf,
    allowed_buf,
    grad_att,
    gp_buf,
    local_buf,
    global_buf,
    moment_buf,
    drift_buf,
    x_recv,
    xsum_buf,
    y_recv,
    sums,
    chip_send,
    chip_recv,
    pair_send,
    pair_recv,
    ring_send,
    ring_recv,
    last_send,
    last_recv,
    load_sem,
    send_sem,
    recv_sem,
    ready_sem,
):
    tokens, width = x_buf.shape
    head = val_buf.shape[1]
    rows = width // (4 * Z)
    half, quarter = rows // 2, rows // 4

    replica = lax.axis_index("replica")
    shard = lax.axis_index("shard")
    my_x, my_y = replica // n_y, lax.rem(replica, n_y)
    side, z, core = shard // 16, lax.rem(shard // 2, Z), lax.rem(shard, 2)
    other = 1 - side

    def at_z(step):
        return lax.rem(z + step + 2 * Z, Z)

    def unit(col, zz, cc):
        return col * 16 + zz * 2 + cc

    to_core = {"shard": unit(side, z, 1 - core)}
    to_side = {"shard": unit(other, z, core)}

    def to_z(way):
        return {"shard": unit(side, at_z(way[0]), core)}

    bit = jnp.where(z == 0, 1, 0)
    ways = ((1 - 2 * bit, bit), (2 * bit - 1, 1 - bit))
    to_x = [{"replica": lax.rem(my_x + k, n_x) * n_y + my_y} for k in range(1, n_x)]
    to_y = [{"replica": my_x * n_y + lax.rem(my_y + k, n_y)} for k in range(1, n_y)]

    def describe(stream, key, src, dst, target):
        return pltpu.make_async_remote_copy(
            src_ref=src,
            dst_ref=dst,
            send_sem=send_sem.at[stream],
            recv_sem=recv_sem.at[key if not isinstance(key, tuple) else lanes(*key)],
            device_id=target,
            device_id_type=pl.DeviceIdType.MESH,
        )

    def send(stream, key, src, dst, target):
        describe(stream, key, src, dst, target).start()

    def arrive(key, dst):
        describe(0, key, dst, dst, to_core).wait_recv()

    def drain(stream, src):
        describe(stream, ("mine", 0), src, src, to_core).wait_send()

    def load(n, src, dst):
        copy = pltpu.make_async_copy(src, dst, load_sem.at[n])
        copy.start()
        return copy

    load_w = load(0, w_hbm, w_buf)

    barrier = pltpu.get_barrier_semaphore()

    def signal(sem, target):
        pl.semaphore_signal(
            sem, inc=1, device_id=target, device_id_type=pl.DeviceIdType.MESH
        )

    near = [(other, z), (side, at_z(1)), (side, at_z(-1))]
    far = [
        {"replica": target["replica"], "shard": unit(side, z, 1)} for target in to_x + to_y
    ]
    for col, zz in near:
        signal(barrier, {"shard": unit(col, zz, 0)})

    @pl.when(core == 1)
    def _():
        signal(barrier, to_core)

    for target in far:
        signal(barrier, target)

    def meet(count, counter, sem):
        @pl.when(core == counter)
        def _():
            pl.semaphore_wait(barrier, count)
            signal(sem, to_core)

        @pl.when(core != counter)
        def _():
            pl.semaphore_wait(sem, 1)

    load_local = load(1, local_hbm, local_buf)
    load_global = load(2, global_hbm, global_buf)
    load_doc = load(4, doc_hbm, doc_buf)
    load_val = load(5, val_hbm, val_buf)
    load_cot = load(6, cot_hbm, cot_buf)
    load_moment = load(7, moment_hbm, moment_buf)
    load_index = load(8, index_hbm, index_buf)

    def span(col, zz, cc, lo, count):
        start = pl.multiple_of(unit(col, zz, cc) * rows + lo, 16)
        return gathered.at[pl.ds(start, count), :]

    load_w.wait()
    span(side, z, core, 0, rows)[...] = w_buf[...].astype(jnp.bfloat16)

    meet(2 * len(near) + 1, 0, ready_sem.at[0])

    def piece(kind, way, d, cc, h):
        zz = at_z(-way[0] * d)
        col = other if kind == KIND_O else side
        lo = 0 if kind == KIND_A else half
        if h is None:
            return span(col, zz, cc, lo, half)
        return span(col, zz, cc, lo + h * quarter, quarter)

    def part(way, q):
        return None if q is None else way[1] if q == 0 else 1 - way[1]

    def side_piece(way, d, cc, col):
        zz = at_z(-way[0] * d)
        if d == 4:
            return span(col, zz, cc, part(way, 0) * quarter, quarter)
        return span(col, zz, cc, 0, half)

    def ring_lane(kind, way, d, q):
        if kind == KIND_B:
            return lanes("ring", kind, d, width=2) + way[1]
        if d == 4:
            return lanes("ring", kind, d, width=2) + way[1]
        return lanes("ring", kind, d, width=4) + 2 * q + way[1]

    def ring_on(kind, way, d, q):
        if d == 3 and q is None:
            q = 0
        if d < 3 or (d == 3 and q == 0):
            src = piece(kind, way, d, core, part(way, q))
            send(RING, ring_lane(kind, way, d + 1, q), src, src, to_z(way))

    def side_on(d, got):
        send(SIDE, ("side", d), got, got, to_side)

    def core_on(name, d, got):
        send(CORE, (name, d), got, got, to_core)

    first_a = span(side, z, core, 0, half)
    for h in (0, 1):
        first_b = span(side, z, core, half + h * quarter, quarter)
        send(SIDE, ("sideB", h), first_b, first_b, to_side)
    for q in (0, 1):
        for way in WAYS:
            ring_on(KIND_A, way, 0, q)
    for way in WAYS:
        ring_on(KIND_B, way, 0, None)
    load_x = load(3, x_hbm, x_buf)

    block = 2 * rows

    def make_drift():
        load_index.wait()
        load_local.wait()
        load_global.wait()
        chosen = index_buf[0]
        current = global_buf[chosen]
        local_rows = local_buf[...].astype(jnp.float32)
        picked = lax.broadcasted_iota(jnp.int32, local_rows.shape, 0) == chosen
        local_copy = jnp.sum(jnp.where(picked, local_rows, 0.0), axis=0, keepdims=True)
        drift_buf[...] = (current - local_copy).astype(jnp.bfloat16).astype(jnp.float32)

    def transpose_block(p):
        cols = slice(p * block, (p + 1) * block)
        turned = x_buf[:, cols].T
        for cc in (0, 1):
            start = pl.multiple_of(p * block + (core if cc == 0 else 1 - core) * rows, 64)
            xt_buf[pl.ds(start, rows), :] = turned[cc * rows : (cc + 1) * rows]

    def make_allowed():
        load_doc.wait()
        by_column = jnp.broadcast_to(doc_buf[...], (tokens, tokens))
        by_row = by_column.T
        row = lax.broadcasted_iota(jnp.int32, (tokens, tokens), 0)
        column = lax.broadcasted_iota(jnp.int32, (tokens, tokens), 1)
        same = (by_row == by_column) & (column <= row)
        allowed_buf[...] = jnp.where(same, 1.0, 0.0)

    def make_grad_att():
        load_val.wait()
        load_cot.wait()
        grad_att[...] = lax.dot_general(
            cot_buf[...],
            val_buf[...],
            (((1,), (1,)), ((), ())),
            preferred_element_type=jnp.float32,
        )

    def multiply(col, zz, first=False):
        start = pl.multiple_of(unit(col, zz, 0) * rows, 128)
        term = jnp.dot(
            x_buf[:, pl.ds(start, block)],
            gathered[pl.ds(start, block), :],
            preferred_element_type=jnp.float32,
        )
        if first:
            proj[...] = term
        else:
            proj[...] += term

    def arrive_core(name, d):
        count = rows if d in (0, 4) else 2 * rows
        arrive((name, d), gathered.at[pl.ds(0, count), :])

    fillers = [make_drift, make_allowed, make_grad_att, load_x.wait]
    fillers += [functools.partial(transpose_block, p) for p in range(2 * Z)]

    def fill(count=1):
        for _ in range(min(count, len(fillers))):
            fillers.pop(0)()

    def queue_products(name, d):
        col = side if name == "mine" else other
        fillers.append(functools.partial(arrive_core, name, d))
        for step, _ in WAYS if 0 < d < 4 else WAYS[:1]:
            fillers.append(
                functools.partial(
                    multiply, col, at_z(-step * d), first=d == 0 and name == "mine"
                )
            )

    def sums_over_x():
        total = drift_buf[...]
        if n_x > 1:
            arrive(("x",), x_recv)
        for k in range(n_x - 1):
            total = total + x_recv[k]
        xsum_buf[...] = total
        for k, target in enumerate(to_y):
            send(ACROSS_Y, ("y",), xsum_buf, y_recv.at[k], target)

    def from_side(d):
        arrive(("side", d), gathered.at[pl.ds(0, half if d in (0, 4) else rows), :])
        for way in WAYS if d else WAYS[:1]:
            core_on("theirs", d, side_piece(way, d, core, other))

    def from_ring(kind, d, q):
        for way in ways:
            got = piece(kind, way, d, core, part(way, 0 if d == 4 else q))
            arrive(ring_lane(kind, way, d, q), got)
            ring_on(kind, way, d, q)
            if kind == KIND_A:
                side_on(d, got)
            core_on("theirs" if kind == KIND_O else "mine", d, got)

    fill(3)
    for d in range(1, 5):
        for h in (0, 1):
            if d < 4 or h == 0:
                from_ring(KIND_A, d, h)
            if d == 1:
                their_b = span(other, z, core, half + h * quarter, quarter)
                arrive(("sideB", h), their_b)
                for way in WAYS:
                    ring_on(KIND_O, way, 0, h if way[1] == 0 else 1 - h)
                core_on("theirs", 0, their_b)
            else:
                from_ring(KIND_O, d - 1, h)
        if d == 1:
            side_on(0, first_a)
            core_on("mine", 0, span(side, z, core, 0, rows))
            queue_products("mine", 0)
        fill(3)
        from_ring(KIND_B, d, None)
        queue_products("mine", d)
        if d == 2 and far:
            meet(2 * len(far), 1, ready_sem.at[1])
            for k, target in enumerate(to_x):
                send(ACROSS_X, ("x",), drift_buf, x_recv.at[k], target)
        if d >= 2:
            from_side(d - 2)
            queue_products("theirs", d - 2)
        fill(5)
    from_side(3)
    queue_products("theirs", 3)
    fill(len(fillers) - 3)
    from_ring(KIND_O, 4, None)
    from_side(4)
    queue_products("theirs", 4)
    fill(len(fillers))
    sums_over_x()

    input_scale = 1.0 / math.sqrt(width)
    score_scale = 1.0 / math.sqrt(head)

    def halves(value):
        high = value.astype(jnp.bfloat16)
        return high, (value - high.astype(jnp.float32)).astype(jnp.bfloat16)

    def product(left, right, left_dim, right_dim):
        dims = (((left_dim,), (right_dim,)), ((), ()))
        terms = ((0, 0), (0, 1), (1, 0))
        return sum(
            lax.dot_general(
                left[i], right[j], dims, preferred_element_type=jnp.float32
            )
            for i, j in terms
        )

    scaled = proj[...] * input_scale
    queries, keys_part = scaled[:, :head], scaled[:, head:]
    q_rate = lax.rsqrt(jnp.mean(queries * queries, axis=1, keepdims=True) + epsilon)
    k_rate = lax.rsqrt(jnp.mean(keys_part * keys_part, axis=1, keepdims=True) + epsilon)
    q_unit, k_unit = queries * q_rate, keys_part * k_rate
    q_parts, k_parts = halves(q_unit), halves(k_unit)
    scores = product(q_parts, k_parts, 1, 1) * score_scale
    raised = jnp.where(allowed_buf[...] > 0.5, jnp.exp(scores), 0.0)
    attention = raised / jnp.sum(raised, axis=1, keepdims=True)
    weighted = attention * grad_att[...]
    grad_scores = (
        weighted - attention * jnp.sum(weighted, axis=1, keepdims=True)
    ) * score_scale
    score_parts = halves(grad_scores)
    grad_qunit = product(score_parts, k_parts, 1, 0)
    grad_kunit = product(score_parts, q_parts, 0, 0)
    grad_query = q_rate * (
        grad_qunit - q_unit * jnp.mean(grad_qunit * q_unit, axis=1, keepdims=True)
    )
    grad_keys = k_rate * (
        grad_kunit - k_unit * jnp.mean(grad_kunit * k_unit, axis=1, keepdims=True)
    )
    gp_buf[:, :head] = (grad_query * input_scale).astype(jnp.bfloat16)
    gp_buf[:, head:] = (grad_keys * input_scale).astype(jnp.bfloat16)

    def place(delta):
        return ORDER.index(delta)

    def compute(delta):
        i, zz = place(delta), at_z(delta)
        for k, col in ((1, other), (0, side)):
            start = pl.multiple_of(unit(col, zz, 0) * rows, 128)
            term = jnp.dot(
                xt_buf[pl.ds(start, block), :],
                gp_buf[...],
                preferred_element_type=jnp.float32,
            )
            chip_send[i, k] = term[rows:].astype(jnp.bfloat16)
            sums[i, k] = term[:rows]
        send(CHIP, ("chip", i), chip_send.at[i], chip_recv.at[i], to_core)

    def pair(delta):
        i = place(delta)
        arrive(("chip", i), chip_recv.at[i])
        for k in (1, 0):
            sums[i, k] += chip_recv[i, k].astype(jnp.float32)
            if k == 1:
                pair_send[i] = sums[i, 1, :half].astype(jnp.bfloat16)
                send(PAIR, ("pair", i), pair_send.at[i], pair_recv.at[i], to_side)

    def across(delta):
        i = place(delta)
        arrive(("pair", i), pair_recv.at[i])
        sums[i, 0, :half] += pair_recv[i].astype(jnp.float32)

    def slot(way, kind, d, late):
        return way[1] * 24 + kind * 8 + (d - 1) * 2 + late

    first_sum = lanes("sum", width=48)

    def ring_sum(kind, way, d, late):
        i = 0 if d == 4 else 1 + 2 * (3 - d) + way[1]
        k = 1 if kind == KIND_O else 0
        h = way[1] if late else 1 - way[1]
        lo = (0 if kind == KIND_A else half) + h * quarter
        total = sums[i, k, pl.ds(pl.multiple_of(lo, 8), quarter)]
        if d < 3 or (d == 3 and late):
            n = slot(way, kind, d + 1, late)
            arrive(first_sum + n, ring_recv.at[n])
            total = total + ring_recv[n].astype(jnp.float32)
        n = slot(way, kind, d, late)
        ring_send[n] = total.astype(jnp.bfloat16)
        send(SUM, first_sum + n, ring_send.at[n], ring_recv.at[n], to_z(way))

    def sum_on(kinds, d, first, among=ways):
        for kind in kinds:
            for way in among:
                ring_sum(kind, way, d, 0 if first else 1)

    whole, split = (KIND_O, KIND_B), (KIND_A,)
    compute(4)
    compute(3)
    pair(4)
    sum_on(whole, 4, False)
    compute(-3)
    compute(2)
    pair(3)
    sum_on(whole, 3, True, WAYS[:1])
    compute(-2)
    pair(-3)
    sum_on(whole, 3, True, WAYS[1:])
    compute(1)
    pair(2)
    compute(-1)
    pair(-2)
    sum_on(whole, 3, False)
    compute(0)
    pair(1)
    across(4)
    sum_on(split, 4, False)
    sum_on(whole, 2, True)
    pair(-1)
    sum_on(whole, 2, False)
    across(3)
    across(-3)
    pair(0)
    sum_on(split, 3, False)
    sum_on(split, 3, True)
    sum_on(whole, 1, True)
    sum_on(whole, 1, False)
    across(2)
    across(-2)
    sum_on(split, 2, False)
    sum_on(split, 2, True)
    across(1)
    across(-1)

    def last_sum(kind, h):
        k = 1 if kind == KIND_O else 0
        lo = (0 if kind == KIND_A else half) + h * quarter
        total = sums[place(0), k, lo : lo + quarter]
        for way in WAYS:
            n = slot(way, kind, 1, 1 if h == way[1] else 0)
            arrive(first_sum + n, ring_recv.at[n])
            total = total + ring_recv[n].astype(jnp.float32)
        return total

    for h in (0, 1):
        last_send[h] = last_sum(KIND_O, h).astype(jnp.bfloat16)
        send(LAST, ("last", h), last_send.at[h], last_recv.at[h], to_side)
    sum_on(split, 1, False)
    sum_on(split, 1, True)
    across(0)

    load_moment.wait()
    chosen = index_buf[0]
    total = xsum_buf[...]
    if n_y > 1:
        arrive(("y",), y_recv)
    for k in range(n_y - 1):
        total = total + y_recv[k]
    drift_mean = total / (n_x * n_y)
    new_moment = outer_momentum * moment_buf[chosen] + drift_mean
    new_global = global_buf[chosen] - outer_rate * (
        drift_mean + outer_momentum * new_moment
    )
    moment_out[...] = new_moment
    global_out[...] = new_global

    for h in (0, 1):
        grad_out[pl.ds(h * quarter, quarter), :] = last_sum(KIND_A, h)
    for h in (0, 1):
        total = last_sum(KIND_B, h)
        arrive(("last", h), last_recv.at[h])
        grad_out[pl.ds(half + h * quarter, quarter), :] = total + last_recv[h].astype(
            jnp.float32
        )
    drain(RING, gathered.at[pl.ds(0, 21 * half), :])
    drain(SIDE, gathered.at[pl.ds(0, 9 * half), :])
    drain(CORE, gathered.at[pl.ds(0, 16 * rows), :])
    drain(CHIP, chip_send)
    drain(PAIR, pair_send)
    drain(SUM, ring_send.at[pl.ds(0, 42)])
    drain(LAST, last_send)
    if n_x > 1:
        drain(ACROSS_X, x_recv)
    if n_y > 1:
        drain(ACROSS_Y, y_recv)


def exchange(n_replica, inputs, doc_ids, values, cotangent, weights, local, current, moment, index):
    tokens, width = inputs.shape
    head = values.shape[1]
    rows = width // (4 * Z)
    half, quarter = rows // 2, rows // 4
    n_x = min(4, n_replica)
    n_y = n_replica // n_x
    bf16, f32 = jnp.bfloat16, jnp.float32
    anywhere = pl.BlockSpec(memory_space=pl.ANY)
    vmem = pl.BlockSpec(memory_space=pltpu.VMEM)
    return pl.pallas_call(
        functools.partial(kernel, n_x, n_y, Lanes()),
        out_shape=(
            jax.ShapeDtypeStruct((rows, 2 * head), f32),
            jax.ShapeDtypeStruct((1, width), f32),
            jax.ShapeDtypeStruct((1, width), f32),
        ),
        in_specs=[pl.BlockSpec(memory_space=pltpu.HBM)] + [anywhere] * 8,
        out_specs=(vmem, vmem, vmem),
        scratch_shapes=[
            pltpu.SMEM((1,), jnp.int32),
            pltpu.VMEM((tokens, width), bf16),
            pltpu.VMEM((width, tokens), bf16),
            pltpu.VMEM((rows, 2 * head), f32),
            pltpu.VMEM((width, 2 * head), bf16),
            pltpu.VMEM((tokens, 2 * head), f32),
            pltpu.VMEM((1, tokens), jnp.int32),
            pltpu.VMEM((tokens, head), bf16),
            pltpu.VMEM((tokens, head), bf16),
            pltpu.VMEM((tokens, tokens), f32),
            pltpu.VMEM((tokens, tokens), f32),
            pltpu.VMEM((tokens, 2 * head), bf16),
            pltpu.VMEM(local.shape, bf16),
            pltpu.VMEM(current.shape, f32),
            pltpu.VMEM(moment.shape, f32),
            pltpu.VMEM((1, width), f32),
            pltpu.VMEM((max(n_x - 1, 1), 1, width), f32),
            pltpu.VMEM((1, width), f32),
            pltpu.VMEM((max(n_y - 1, 1), 1, width), f32),
            pltpu.VMEM((8, 2, rows, 2 * head), f32),
            pltpu.VMEM((8, 2, rows, 2 * head), bf16),
            pltpu.VMEM((8, 2, rows, 2 * head), bf16),
            pltpu.VMEM((8, half, 2 * head), bf16),
            pltpu.VMEM((8, half, 2 * head), bf16),
            pltpu.VMEM((48, quarter, 2 * head), bf16),
            pltpu.VMEM((48, quarter, 2 * head), bf16),
            pltpu.VMEM((2, quarter, 2 * head), bf16),
            pltpu.VMEM((2, quarter, 2 * head), bf16),
            pltpu.SemaphoreType.DMA((9,)),
            pltpu.SemaphoreType.DMA((9,)),
            pltpu.SemaphoreType.DMA((124,)),
            pltpu.SemaphoreType.REGULAR((2,)),
        ],
        compiler_params=pltpu.CompilerParams(
            collective_id=0, has_side_effects=True, vmem_limit_bytes=56 * 1024 * 1024
        ),
    )(index, inputs, doc_ids, values, cotangent, weights, local, current, moment)


def finish(
    grad, weights, moment1, moment2, new_global, new_moment, out_w, out_1, out_2, out_g, out_m
):
    gradient, rows = grad[...], weights[...]
    first_new = beta_one * moment1[...] + (1.0 - beta_one) * gradient
    second_new = beta_two * moment2[...] + (1.0 - beta_two) * gradient * gradient
    first_hat = first_new / (1.0 - beta_one**ADAM_STEP)
    second_hat = second_new / (1.0 - beta_two**ADAM_STEP)
    out_w[...] = rows - learn_rate * (
        first_hat / (jnp.sqrt(second_hat) + 1e-08) + decay_rate * rows
    )
    out_1[...] = first_new
    out_2[...] = second_new
    out_g[...] = new_global[...]
    out_m[...] = new_moment[...]


def on_device(
    n_replica,
    inputs,
    doc_ids,
    values,
    cotangent,
    weights,
    moment1,
    moment2,
    frag_local,
    frag_global,
    frag_moment,
    frag_index,
):
    gradient, new_global, new_moment = exchange(
        n_replica,
        inputs,
        doc_ids,
        values,
        cotangent,
        weights,
        frag_local[0, :, 0, :],
        frag_global,
        frag_moment,
        frag_index,
    )
    vmem = pl.BlockSpec(memory_space=pltpu.VMEM)
    like = jax.ShapeDtypeStruct(weights.shape, jnp.float32)
    row = jax.ShapeDtypeStruct(new_global.shape, jnp.float32)
    return pl.pallas_call(
        finish,
        out_shape=(like, like, like, row, row),
        in_specs=[vmem] * 6,
        out_specs=(vmem,) * 5,
    )(gradient, weights, moment1, moment2, new_global, new_moment)


def solution(mesh):
    both = P(("replica", "shard"), None)
    return jax.shard_map(
        functools.partial(on_device, mesh.shape["replica"]),
        mesh=mesh,
        in_specs=(both,) * 7
        + (
            P("replica", None, "shard", None),
            P(None, "shard", None),
            P(None, "shard", None),
            P(),
        ),
        out_specs=(both, both, both, P("shard", None), P("shard", None)),
        check_vma=False,
    )
```

```python
import functools
import math

import jax
import jax.numpy as jnp
from jax import lax
from jax.experimental import pallas as pl
from jax.experimental.pallas import tpu as pltpu
from jax.sharding import PartitionSpec as P

ADAM_STEP = 100

epsilon = 1e-06
beta_one = 0.9
beta_two = 0.95
learn_rate = 0.01
decay_rate = 0.1
outer_momentum = 0.9
outer_rate = 0.7

Z = 8
WAYS = ((1, 0), (-1, 1))
KIND_A, KIND_B, KIND_O = 0, 1, 2
RING, SIDE, CORE, CHIP, PAIR, SUM, LAST, ACROSS_X, ACROSS_Y = range(9)
ORDER = (4, 3, -3, 2, -2, 1, -1, 0)


class Lanes:
    def __init__(self):
        self.numbers = {}
        self.count = 0

    def __call__(self, *key, width=1):
        if key not in self.numbers:
            self.numbers[key] = self.count
            self.count += width
        return self.numbers[key]


def kernel(
    n_x,
    n_y,
    lanes,
    index_hbm,
    x_hbm,
    doc_hbm,
    val_hbm,
    cot_hbm,
    w_hbm,
    local_hbm,
    global_hbm,
    moment_hbm,
    grad_out,
    global_out,
    moment_out,
    index_buf,
    x_buf,
    xt_buf,
    w_buf,
    gathered,
    proj,
    doc_buf,
    val_buf,
    cot_buf,
    allowed_buf,
    grad_att,
    gp_buf,
    local_buf,
    global_buf,
    moment_buf,
    drift_buf,
    x_recv,
    xsum_buf,
    y_recv,
    sums,
    chip_send,
    chip_recv,
    pair_send,
    pair_recv,
    ring_send,
    ring_recv,
    last_send,
    last_recv,
    load_sem,
    send_sem,
    recv_sem,
    ready_sem,
):
    tokens, width = x_buf.shape
    head = val_buf.shape[1]
    rows = width // (4 * Z)
    half, quarter = rows // 2, rows // 4

    replica = lax.axis_index("replica")
    shard = lax.axis_index("shard")
    my_x, my_y = replica // n_y, lax.rem(replica, n_y)
    side, z, core = shard // 16, lax.rem(shard // 2, Z), lax.rem(shard, 2)
    other = 1 - side

    def at_z(step):
        return lax.rem(z + step + 2 * Z, Z)

    def unit(col, zz, cc):
        return col * 16 + zz * 2 + cc

    to_core = {"shard": unit(side, z, 1 - core)}
    to_side = {"shard": unit(other, z, core)}

    def to_z(way):
        return {"shard": unit(side, at_z(way[0]), core)}

    bit = jnp.where(z == 0, 1, 0)
    ways = ((1 - 2 * bit, bit), (2 * bit - 1, 1 - bit))
    to_x = [{"replica": lax.rem(my_x + k, n_x) * n_y + my_y} for k in range(1, n_x)]
    to_y = [{"replica": my_x * n_y + lax.rem(my_y + k, n_y)} for k in range(1, n_y)]

    def describe(stream, key, src, dst, target):
        return pltpu.make_async_remote_copy(
            src_ref=src,
            dst_ref=dst,
            send_sem=send_sem.at[stream],
            recv_sem=recv_sem.at[key if not isinstance(key, tuple) else lanes(*key)],
            device_id=target,
            device_id_type=pl.DeviceIdType.MESH,
        )

    def send(stream, key, src, dst, target):
        describe(stream, key, src, dst, target).start()

    def arrive(key, dst):
        describe(0, key, dst, dst, to_core).wait_recv()

    def drain(stream, src):
        describe(stream, ("mine", 0), src, src, to_core).wait_send()

    def load(n, src, dst):
        copy = pltpu.make_async_copy(src, dst, load_sem.at[n])
        copy.start()
        return copy

    load_w = load(0, w_hbm, w_buf)

    barrier = pltpu.get_barrier_semaphore()

    def signal(sem, target):
        pl.semaphore_signal(
            sem, inc=1, device_id=target, device_id_type=pl.DeviceIdType.MESH
        )

    near = [(other, z), (side, at_z(1)), (side, at_z(-1))]
    far = [
        {"replica": target["replica"], "shard": unit(side, z, 1)} for target in to_x + to_y
    ]
    for col, zz in near:
        signal(barrier, {"shard": unit(col, zz, 0)})

    @pl.when(core == 1)
    def _():
        signal(barrier, to_core)

    for target in far:
        signal(barrier, target)

    def meet(count, counter, sem):
        @pl.when(core == counter)
        def _():
            pl.semaphore_wait(barrier, count)
            signal(sem, to_core)

        @pl.when(core != counter)
        def _():
            pl.semaphore_wait(sem, 1)

    load_local = load(1, local_hbm, local_buf)
    load_global = load(2, global_hbm, global_buf)
    load_doc = load(4, doc_hbm, doc_buf)
    load_val = load(5, val_hbm, val_buf)
    load_cot = load(6, cot_hbm, cot_buf)
    load_moment = load(7, moment_hbm, moment_buf)
    load_index = load(8, index_hbm, index_buf)

    def span(col, zz, cc, lo, count):
        start = pl.multiple_of(unit(col, zz, cc) * rows + lo, 16)
        return gathered.at[pl.ds(start, count), :]

    load_w.wait()
    span(side, z, core, 0, rows)[...] = w_buf[...].astype(jnp.bfloat16)

    meet(2 * len(near) + 1, 0, ready_sem.at[0])

    def piece(kind, way, d, cc, h):
        zz = at_z(-way[0] * d)
        col = other if kind == KIND_O else side
        lo = 0 if kind == KIND_A else half
        if h is None:
            return span(col, zz, cc, lo, half)
        return span(col, zz, cc, lo + h * quarter, quarter)

    def part(way, q):
        return None if q is None else way[1] if q == 0 else 1 - way[1]

    def side_piece(way, d, cc, col):
        zz = at_z(-way[0] * d)
        if d == 4:
            return span(col, zz, cc, part(way, 0) * quarter, quarter)
        return span(col, zz, cc, 0, half)

    def ring_lane(kind, way, d, q):
        if kind == KIND_B:
            return lanes("ring", kind, d, width=2) + way[1]
        if d == 4:
            return lanes("ring", kind, d, width=2) + way[1]
        return lanes("ring", kind, d, width=4) + 2 * q + way[1]

    def ring_on(kind, way, d, q):
        if d == 3 and q is None:
            q = 0
        if d < 3 or (d == 3 and q == 0):
            src = piece(kind, way, d, core, part(way, q))
            send(RING, ring_lane(kind, way, d + 1, q), src, src, to_z(way))

    def side_on(d, got):
        send(SIDE, ("side", d), got, got, to_side)

    def core_on(name, d, got):
        send(CORE, (name, d), got, got, to_core)

    first_a = span(side, z, core, 0, half)
    for h in (0, 1):
        first_b = span(side, z, core, half + h * quarter, quarter)
        send(SIDE, ("sideB", h), first_b, first_b, to_side)
    for q in (0, 1):
        for way in WAYS:
            ring_on(KIND_A, way, 0, q)
    for way in WAYS:
        ring_on(KIND_B, way, 0, None)
    load_x = load(3, x_hbm, x_buf)

    block = 2 * rows

    def make_drift():
        load_index.wait()
        load_local.wait()
        load_global.wait()
        chosen = index_buf[0]
        current = global_buf[chosen]
        local_rows = local_buf[...].astype(jnp.float32)
        picked = lax.broadcasted_iota(jnp.int32, local_rows.shape, 0) == chosen
        local_copy = jnp.sum(jnp.where(picked, local_rows, 0.0), axis=0, keepdims=True)
        drift_buf[...] = (current - local_copy).astype(jnp.bfloat16).astype(jnp.float32)

    def transpose_block(p):
        cols = slice(p * block, (p + 1) * block)
        turned = x_buf[:, cols].T
        for cc in (0, 1):
            start = pl.multiple_of(p * block + (core if cc == 0 else 1 - core) * rows, 64)
            xt_buf[pl.ds(start, rows), :] = turned[cc * rows : (cc + 1) * rows]

    def make_allowed():
        load_doc.wait()
        by_column = jnp.broadcast_to(doc_buf[...], (tokens, tokens))
        by_row = by_column.T
        row = lax.broadcasted_iota(jnp.int32, (tokens, tokens), 0)
        column = lax.broadcasted_iota(jnp.int32, (tokens, tokens), 1)
        same = (by_row == by_column) & (column <= row)
        allowed_buf[...] = jnp.where(same, 1.0, 0.0)

    def make_grad_att():
        load_val.wait()
        load_cot.wait()
        grad_att[...] = lax.dot_general(
            cot_buf[...],
            val_buf[...],
            (((1,), (1,)), ((), ())),
            preferred_element_type=jnp.float32,
        )

    def multiply(col, zz, first=False):
        start = pl.multiple_of(unit(col, zz, 0) * rows, 128)
        term = jnp.dot(
            x_buf[:, pl.ds(start, block)],
            gathered[pl.ds(start, block), :],
            preferred_element_type=jnp.float32,
        )
        if first:
            proj[...] = term
        else:
            proj[...] += term

    def arrive_core(name, d):
        count = rows if d in (0, 4) else 2 * rows
        arrive((name, d), gathered.at[pl.ds(0, count), :])

    fillers = [make_drift, make_allowed, make_grad_att, load_x.wait]
    fillers += [functools.partial(transpose_block, p) for p in range(2 * Z)]

    def fill(count=1):
        for _ in range(min(count, len(fillers))):
            fillers.pop(0)()

    def queue_products(name, d):
        col = side if name == "mine" else other
        fillers.append(functools.partial(arrive_core, name, d))
        for step, _ in WAYS if 0 < d < 4 else WAYS[:1]:
            fillers.append(
                functools.partial(
                    multiply, col, at_z(-step * d), first=d == 0 and name == "mine"
                )
            )

    def sums_over_x():
        total = drift_buf[...]
        if n_x > 1:
            arrive(("x",), x_recv)
        for k in range(n_x - 1):
            total = total + x_recv[k]
        xsum_buf[...] = total
        for k, target in enumerate(to_y):
            send(ACROSS_Y, ("y",), xsum_buf, y_recv.at[k], target)

    def from_side(d):
        arrive(("side", d), gathered.at[pl.ds(0, half if d in (0, 4) else rows), :])
        for way in WAYS if d else WAYS[:1]:
            core_on("theirs", d, side_piece(way, d, core, other))

    def from_ring(kind, d, q):
        for way in ways:
            got = piece(kind, way, d, core, part(way, 0 if d == 4 else q))
            arrive(ring_lane(kind, way, d, q), got)
            ring_on(kind, way, d, q)
            if kind == KIND_A:
                side_on(d, got)
            core_on("theirs" if kind == KIND_O else "mine", d, got)

    fill(3)
    for d in range(1, 5):
        for h in (0, 1):
            if d < 4 or h == 0:
                from_ring(KIND_A, d, h)
            if d == 1:
                their_b = span(other, z, core, half + h * quarter, quarter)
                arrive(("sideB", h), their_b)
                for way in WAYS:
                    ring_on(KIND_O, way, 0, h if way[1] == 0 else 1 - h)
                core_on("theirs", 0, their_b)
            else:
                from_ring(KIND_O, d - 1, h)
        if d == 1:
            side_on(0, first_a)
            core_on("mine", 0, span(side, z, core, 0, rows))
            queue_products("mine", 0)
        fill(3)
        from_ring(KIND_B, d, None)
        queue_products("mine", d)
        if d == 2 and far:
            meet(2 * len(far), 1, ready_sem.at[1])
            for k, target in enumerate(to_x):
                send(ACROSS_X, ("x",), drift_buf, x_recv.at[k], target)
        if d >= 2:
            from_side(d - 2)
            queue_products("theirs", d - 2)
        fill(5)
    from_side(3)
    queue_products("theirs", 3)
    fill(len(fillers) - 3)
    from_ring(KIND_O, 4, None)
    from_side(4)
    queue_products("theirs", 4)
    fill(len(fillers))
    sums_over_x()

    input_scale = 1.0 / math.sqrt(width)
    score_scale = 1.0 / math.sqrt(head)

    def halves(value):
        high = value.astype(jnp.bfloat16)
        return high, (value - high.astype(jnp.float32)).astype(jnp.bfloat16)

    def product(left, right, left_dim, right_dim):
        dims = (((left_dim,), (right_dim,)), ((), ()))
        terms = ((0, 0), (0, 1), (1, 0))
        return sum(
            lax.dot_general(
                left[i], right[j], dims, preferred_element_type=jnp.float32
            )
            for i, j in terms
        )

    scaled = proj[...] * input_scale
    queries, keys_part = scaled[:, :head], scaled[:, head:]
    q_rate = lax.rsqrt(jnp.mean(queries * queries, axis=1, keepdims=True) + epsilon)
    k_rate = lax.rsqrt(jnp.mean(keys_part * keys_part, axis=1, keepdims=True) + epsilon)
    q_unit, k_unit = queries * q_rate, keys_part * k_rate
    q_parts, k_parts = halves(q_unit), halves(k_unit)
    scores = product(q_parts, k_parts, 1, 1) * score_scale
    raised = jnp.where(allowed_buf[...] > 0.5, jnp.exp(scores), 0.0)
    attention = raised / jnp.sum(raised, axis=1, keepdims=True)
    weighted = attention * grad_att[...]
    grad_scores = (
        weighted - attention * jnp.sum(weighted, axis=1, keepdims=True)
    ) * score_scale
    score_parts = halves(grad_scores)
    grad_qunit = product(score_parts, k_parts, 1, 0)
    grad_kunit = product(score_parts, q_parts, 0, 0)
    grad_query = q_rate * (
        grad_qunit - q_unit * jnp.mean(grad_qunit * q_unit, axis=1, keepdims=True)
    )
    grad_keys = k_rate * (
        grad_kunit - k_unit * jnp.mean(grad_kunit * k_unit, axis=1, keepdims=True)
    )
    gp_buf[:, :head] = (grad_query * input_scale).astype(jnp.bfloat16)
    gp_buf[:, head:] = (grad_keys * input_scale).astype(jnp.bfloat16)

    def place(delta):
        return ORDER.index(delta)

    def compute(delta):
        i, zz = place(delta), at_z(delta)
        for k, col in ((1, other), (0, side)):
            start = pl.multiple_of(unit(col, zz, 0) * rows, 128)
            term = jnp.dot(
                xt_buf[pl.ds(start, block), :],
                gp_buf[...],
                preferred_element_type=jnp.float32,
            )
            chip_send[i, k] = term[rows:].astype(jnp.bfloat16)
            sums[i, k] = term[:rows]
        send(CHIP, ("chip", i), chip_send.at[i], chip_recv.at[i], to_core)

    def compute_first():
        both = ((1, other), (0, side))
        starts = [unit(col, at_z(4), 0) * rows for _, col in both]
        for (k, _), start in zip(both, starts):
            chip_send[0, k] = jnp.dot(
                xt_buf[pl.ds(pl.multiple_of(start + rows, 64), rows), :],
                gp_buf[...],
                preferred_element_type=jnp.float32,
            ).astype(jnp.bfloat16)
        send(CHIP, ("chip", 0), chip_send.at[0], chip_recv.at[0], to_core)
        for (k, _), start in zip(both, starts):
            sums[0, k] = jnp.dot(
                xt_buf[pl.ds(pl.multiple_of(start, 128), rows), :],
                gp_buf[...],
                preferred_element_type=jnp.float32,
            )

    def pair(delta):
        i = place(delta)
        arrive(("chip", i), chip_recv.at[i])
        for k in (1, 0):
            sums[i, k] += chip_recv[i, k].astype(jnp.float32)
            if k == 1:
                pair_send[i] = sums[i, 1, :half].astype(jnp.bfloat16)
                send(PAIR, ("pair", i), pair_send.at[i], pair_recv.at[i], to_side)

    def across(delta):
        i = place(delta)
        arrive(("pair", i), pair_recv.at[i])
        sums[i, 0, :half] += pair_recv[i].astype(jnp.float32)

    def slot(way, kind, d, late):
        return way[1] * 24 + kind * 8 + (d - 1) * 2 + late

    first_sum = lanes("sum", width=48)

    def ring_sum(kind, way, d, late):
        i = 0 if d == 4 else 1 + 2 * (3 - d) + way[1]
        k = 1 if kind == KIND_O else 0
        h = way[1] if late else 1 - way[1]
        lo = (0 if kind == KIND_A else half) + h * quarter
        total = sums[i, k, pl.ds(pl.multiple_of(lo, 8), quarter)]
        if d < 3 or (d == 3 and late):
            n = slot(way, kind, d + 1, late)
            arrive(first_sum + n, ring_recv.at[n])
            total = total + ring_recv[n].astype(jnp.float32)
        n = slot(way, kind, d, late)
        ring_send[n] = total.astype(jnp.bfloat16)
        send(SUM, first_sum + n, ring_send.at[n], ring_recv.at[n], to_z(way))

    def sum_on(kinds, d, first, among=ways):
        for kind in kinds:
            for way in among:
                ring_sum(kind, way, d, 0 if first else 1)

    whole, split = (KIND_O, KIND_B), (KIND_A,)
    compute_first()
    compute(3)
    pair(4)
    sum_on(whole, 4, False)
    compute(-3)
    compute(2)
    pair(3)
    sum_on(whole, 3, True, WAYS[:1])
    compute(-2)
    pair(-3)
    sum_on(whole, 3, True, WAYS[1:])
    compute(1)
    pair(2)
    compute(-1)
    pair(-2)
    sum_on(whole, 3, False)
    compute(0)
    pair(1)
    across(4)
    sum_on(split, 4, False)
    sum_on(whole, 2, True)
    pair(-1)
    sum_on(whole, 2, False)
    across(3)
    across(-3)
    pair(0)
    sum_on(split, 3, False)
    sum_on(split, 3, True)
    sum_on(whole, 1, True)
    sum_on(whole, 1, False)
    across(2)
    across(-2)
    sum_on(split, 2, False)
    sum_on(split, 2, True)
    across(1)
    across(-1)

    def last_sum(kind, h):
        k = 1 if kind == KIND_O else 0
        lo = (0 if kind == KIND_A else half) + h * quarter
        total = sums[place(0), k, lo : lo + quarter]
        for way in WAYS:
            n = slot(way, kind, 1, 1 if h == way[1] else 0)
            arrive(first_sum + n, ring_recv.at[n])
            total = total + ring_recv[n].astype(jnp.float32)
        return total

    for h in (0, 1):
        last_send[h] = last_sum(KIND_O, h).astype(jnp.bfloat16)
        send(LAST, ("last", h), last_send.at[h], last_recv.at[h], to_side)
    sum_on(split, 1, False)
    sum_on(split, 1, True)
    across(0)

    load_moment.wait()
    chosen = index_buf[0]
    total = xsum_buf[...]
    if n_y > 1:
        arrive(("y",), y_recv)
    for k in range(n_y - 1):
        total = total + y_recv[k]
    drift_mean = total / (n_x * n_y)
    new_moment = outer_momentum * moment_buf[chosen] + drift_mean
    new_global = global_buf[chosen] - outer_rate * (
        drift_mean + outer_momentum * new_moment
    )
    moment_out[...] = new_moment
    global_out[...] = new_global

    for h in (0, 1):
        grad_out[pl.ds(h * quarter, quarter), :] = last_sum(KIND_A, h)
    for h in (0, 1):
        total = last_sum(KIND_B, h)
        arrive(("last", h), last_recv.at[h])
        grad_out[pl.ds(half + h * quarter, quarter), :] = total + last_recv[h].astype(
            jnp.float32
        )
    drain(RING, gathered.at[pl.ds(0, 21 * half), :])
    drain(SIDE, gathered.at[pl.ds(0, 9 * half), :])
    drain(CORE, gathered.at[pl.ds(0, 16 * rows), :])
    drain(CHIP, chip_send)
    drain(PAIR, pair_send)
    drain(SUM, ring_send.at[pl.ds(0, 42)])
    drain(LAST, last_send)
    if n_x > 1:
        drain(ACROSS_X, x_recv)
    if n_y > 1:
        drain(ACROSS_Y, y_recv)


def exchange(n_replica, inputs, doc_ids, values, cotangent, weights, local, current, moment, index):
    tokens, width = inputs.shape
    head = values.shape[1]
    rows = width // (4 * Z)
    half, quarter = rows // 2, rows // 4
    n_x = min(4, n_replica)
    n_y = n_replica // n_x
    bf16, f32 = jnp.bfloat16, jnp.float32
    anywhere = pl.BlockSpec(memory_space=pl.ANY)
    vmem = pl.BlockSpec(memory_space=pltpu.VMEM)
    return pl.pallas_call(
        functools.partial(kernel, n_x, n_y, Lanes()),
        out_shape=(
            jax.ShapeDtypeStruct((rows, 2 * head), f32),
            jax.ShapeDtypeStruct((1, width), f32),
            jax.ShapeDtypeStruct((1, width), f32),
        ),
        in_specs=[pl.BlockSpec(memory_space=pltpu.HBM)] + [anywhere] * 8,
        out_specs=(vmem, vmem, vmem),
        scratch_shapes=[
            pltpu.SMEM((1,), jnp.int32),
            pltpu.VMEM((tokens, width), bf16),
            pltpu.VMEM((width, tokens), bf16),
            pltpu.VMEM((rows, 2 * head), f32),
            pltpu.VMEM((width, 2 * head), bf16),
            pltpu.VMEM((tokens, 2 * head), f32),
            pltpu.VMEM((1, tokens), jnp.int32),
            pltpu.VMEM((tokens, head), bf16),
            pltpu.VMEM((tokens, head), bf16),
            pltpu.VMEM((tokens, tokens), f32),
            pltpu.VMEM((tokens, tokens), f32),
            pltpu.VMEM((tokens, 2 * head), bf16),
            pltpu.VMEM(local.shape, bf16),
            pltpu.VMEM(current.shape, f32),
            pltpu.VMEM(moment.shape, f32),
            pltpu.VMEM((1, width), f32),
            pltpu.VMEM((max(n_x - 1, 1), 1, width), f32),
            pltpu.VMEM((1, width), f32),
            pltpu.VMEM((max(n_y - 1, 1), 1, width), f32),
            pltpu.VMEM((8, 2, rows, 2 * head), f32),
            pltpu.VMEM((8, 2, rows, 2 * head), bf16),
            pltpu.VMEM((8, 2, rows, 2 * head), bf16),
            pltpu.VMEM((8, half, 2 * head), bf16),
            pltpu.VMEM((8, half, 2 * head), bf16),
            pltpu.VMEM((48, quarter, 2 * head), bf16),
            pltpu.VMEM((48, quarter, 2 * head), bf16),
            pltpu.VMEM((2, quarter, 2 * head), bf16),
            pltpu.VMEM((2, quarter, 2 * head), bf16),
            pltpu.SemaphoreType.DMA((9,)),
            pltpu.SemaphoreType.DMA((9,)),
            pltpu.SemaphoreType.DMA((124,)),
            pltpu.SemaphoreType.REGULAR((2,)),
        ],
        compiler_params=pltpu.CompilerParams(
            collective_id=0, has_side_effects=True, vmem_limit_bytes=56 * 1024 * 1024
        ),
    )(index, inputs, doc_ids, values, cotangent, weights, local, current, moment)


def finish(
    grad, weights, moment1, moment2, new_global, new_moment, out_w, out_1, out_2, out_g, out_m
):
    gradient, rows = grad[...], weights[...]
    first_new = beta_one * moment1[...] + (1.0 - beta_one) * gradient
    second_new = beta_two * moment2[...] + (1.0 - beta_two) * gradient * gradient
    first_hat = first_new / (1.0 - beta_one**ADAM_STEP)
    second_hat = second_new / (1.0 - beta_two**ADAM_STEP)
    out_w[...] = rows - learn_rate * (
        first_hat / (jnp.sqrt(second_hat) + 1e-08) + decay_rate * rows
    )
    out_1[...] = first_new
    out_2[...] = second_new
    out_g[...] = new_global[...]
    out_m[...] = new_moment[...]


def on_device(
    n_replica,
    inputs,
    doc_ids,
    values,
    cotangent,
    weights,
    moment1,
    moment2,
    frag_local,
    frag_global,
    frag_moment,
    frag_index,
):
    gradient, new_global, new_moment = exchange(
        n_replica,
        inputs,
        doc_ids,
        values,
        cotangent,
        weights,
        frag_local[0, :, 0, :],
        frag_global,
        frag_moment,
        frag_index,
    )
    vmem = pl.BlockSpec(memory_space=pltpu.VMEM)
    like = jax.ShapeDtypeStruct(weights.shape, jnp.float32)
    row = jax.ShapeDtypeStruct(new_global.shape, jnp.float32)
    return pl.pallas_call(
        finish,
        out_shape=(like, like, like, row, row),
        in_specs=[vmem] * 6,
        out_specs=(vmem,) * 5,
    )(gradient, weights, moment1, moment2, new_global, new_moment)


def solution(mesh):
    both = P(("replica", "shard"), None)
    return jax.shard_map(
        functools.partial(on_device, mesh.shape["replica"]),
        mesh=mesh,
        in_specs=(both,) * 7
        + (
            P("replica", None, "shard", None),
            P(None, "shard", None),
            P(None, "shard", None),
            P(),
        ),
        out_specs=(both, both, both, P("shard", None), P("shard", None)),
        check_vma=False,
    )
```
